32 devices in a mesh: dp: 4 (over y, x), expert: 8 (over z, core).
Axes of the slice: x: 2, y: 2, z: 4, core: 2. Of those that a mesh axis runs over, the one named last changes fastest.
Arguments:
- tokens: bfloat16 [1024, 2048], P(('dp', 'expert')), may hold values from -6 to 6
- grad_out: bfloat16 [1024, 2048], P(('dp', 'expert')), may hold values from -0.59765625 to 0.59765625
- routing: int32 [1024, 8], P(('dp', 'expert')), may hold values from 0 to 15, as said below
- replica: int32 [1024, 8], P(('dp', 'expert')), may hold values from 0 to 1, as said below
- gates: bfloat16 [1024, 8], P(('dp', 'expert')), may hold values from 0.25 to 4
- host_expert: int32 [8], replicated, may hold values from 0 to 15, as said below
- w_gate_up: bfloat16 [16, 2, 768, 2048], P('expert', None, 'dp'), may hold values from -0.125 to 0.125
- w_down: bfloat16 [16, 768, 2048], P('expert', 'dp'), may hold values from -0.21875 to 0.21875
Outputs:
- grad_tokens: bfloat16 [1024, 2048], P(('dp', 'expert'))
- grad_gates: float32 [1024, 8], P(('dp', 'expert'))
- grad_w_gate_up: bfloat16 [16, 2, 768, 2048], P('expert', None, 'dp')
- grad_w_down: bfloat16 [16, 768, 2048], P('expert', 'dp')
The draws below stay inside these ranges and needn't reach their ends.
Inputs may be any that keep to these rules, and one draw needn't show every extreme that they name: `routing`: column k of a token names an expert of 2 * k to 2 * k + 1. Within the rows of one device, experts 2 i and 2 i + 1 are named together exactly 2 * 16 times. `replica`: within the rows of one device, each expert has at most 16 choices marked 0 and at most 16 marked 1; some expert reaches 16 marked 0 from every device, and in every index of dp some expert reaches 16 marked 1 from every device. Only experts listed in host_expert have choices marked 1. `host_expert`: for every device d of the expert axis exactly one of its experts 2 d and 2 d + 1 is listed, and it is listed once.
All inputs are finite; a program needn't handle non-finite values.
Results may differ from the reference program's by a relative error of at most 0.013.
Values may be sent and summed in bfloat16 or wider, within the bound.
A program may use at most 128 MiB of HBM per device.

```python
import jax
import jax.numpy as jnp
from jax import lax

D = 2048
FF = 768
TOPK = 8
TOK_DEV = 32
EXPERTS = 16
TOKENS = 1024
BAND = 2
SLOT = 16
BLOCK = 128
N_DP = 4
N_EXPERT = 8


def routing_layout(key):
    root_key = jax.random.fold_in(key, 4242)
    subkeys = jax.random.split(root_key, 5)
    pairs_all = N_EXPERT
    plus_bit = jax.random.randint(subkeys[0], (pairs_all,), 0, 2).astype(jnp.int32)
    extra_share = jax.random.randint(subkeys[1], (N_DP, N_EXPERT, pairs_all), 0, SLOT + 1).astype(jnp.int32)
    full_pair = jax.random.randint(subkeys[2], (N_DP, 1, 1), 0, pairs_all).astype(jnp.int32)
    pair_iota = lax.broadcasted_iota(jnp.int32, (N_DP, N_EXPERT, pairs_all), 2)
    extra_share = jnp.where(pair_iota == full_pair, SLOT, extra_share)
    layout_shape = (N_DP, N_EXPERT, TOPK, TOK_DEV)
    position = lax.broadcasted_iota(jnp.int32, layout_shape, 3)
    column = lax.broadcasted_iota(jnp.int32, layout_shape, 2)
    pair_ids = column * (BAND // 2) + position // (2 * SLOT)
    within = position % (2 * SLOT)
    extra_rows = jnp.take_along_axis(extra_share, pair_ids.reshape(N_DP, N_EXPERT, TOPK * TOK_DEV), axis=2).reshape(layout_shape)
    plus_side = within < SLOT + extra_rows
    chosen_bit = jnp.take(plus_bit, pair_ids)
    expert = 2 * pair_ids + jnp.where(plus_side, chosen_bit, 1 - chosen_bit)
    copy_flag = ((within >= SLOT) & plus_side).astype(jnp.int32)
    scores = jax.random.randint(subkeys[3], layout_shape, 0, 1048576).astype(jnp.int32) * TOK_DEV + position
    ordering = jnp.argsort(scores, axis=3, stable=True).astype(jnp.int32)
    expert = jnp.take_along_axis(expert, ordering, axis=3)
    copy_flag = jnp.take_along_axis(copy_flag, ordering, axis=3)
    routing = jnp.transpose(expert, (0, 1, 3, 2)).reshape(N_DP * N_EXPERT * TOK_DEV, TOPK).astype(jnp.int32)
    replica = jnp.transpose(copy_flag, (0, 1, 3, 2)).reshape(N_DP * N_EXPERT * TOK_DEV, TOPK).astype(jnp.int32)
    owners = jax.random.permutation(subkeys[4], N_EXPERT).astype(jnp.int32)
    host_list = (2 * owners + jnp.take(plus_bit, owners)).astype(jnp.int32)
    return (routing, replica, host_list)


def draw_routing(key, part):
    return routing_layout(key)[0]


def draw_replica(key, part):
    return routing_layout(key)[1]


def draw_host_expert(key, part):
    return routing_layout(key)[2]


def level_of(key, shape, cuts, low, top_value):
    loudness = 1.0
    for axis_at, shards_of in cuts:
        heights = jax.random.uniform(jax.random.fold_in(jax.random.fold_in(key, 6), axis_at), (shards_of,), jnp.float32, low / len(cuts), top_value / len(cuts))
        loudness = loudness * jnp.repeat(jnp.exp(heights), shape[axis_at] // shards_of).reshape((-1,) + (1,) * (len(shape) - 1 - axis_at))
    return loudness


def gaussian(stream_key, shape, deviation, most, pieces=(), kind=jnp.bfloat16):
    drawn = jax.random.normal(stream_key, shape, jnp.float32) * deviation
    if len(pieces) > 0:
        drawn = level_of(stream_key, shape, pieces, -0.22, 0.18) * drawn
    return jnp.clip(drawn, min=-most, max=most).astype(kind)


def setup_inputs(seed: int = 0) -> dict:
    key_list = jax.random.split(jax.random.key(seed), 9)
    return {
        "tokens": gaussian(key_list[0], (TOKENS, D), 1.0, 6.0, ((0, 32),)),
        "grad_out": gaussian(key_list[1], (TOKENS, D), 0.1, 0.59765625, ((0, 32),)),
        "routing": draw_routing(jax.random.fold_in(key_list[8], 71), 0),
        "replica": draw_replica(jax.random.fold_in(key_list[8], 71), 0),
        "gates": jnp.clip(0.25 + 3.75 * jax.random.uniform(key_list[4], (TOKENS, TOPK), jnp.float32) ** level_of(key_list[4], (TOKENS, TOPK), ((0, 32),), -0.2, 0.2), 0.25, 4.0).astype(jnp.bfloat16),
        "host_expert": draw_host_expert(jax.random.fold_in(key_list[8], 71), 0),
        "w_gate_up": gaussian(key_list[6], (EXPERTS, 2, FF, D), D ** -0.5, 0.125, ((0, 8), (2, 4))),
        "w_down": gaussian(key_list[7], (EXPERTS, FF, D), FF ** -0.5, 0.21875, ((0, 8), (1, 4))),
    }


def expert_pass(tokens, grad_out, gates, row_ids, live_rows, gate_up_w, down_w):
    token_ids = row_ids // TOPK
    live_mask = live_rows.astype(tokens.dtype)
    inputs = tokens[token_ids] * live_mask[:, None]
    upstream = grad_out[token_ids] * live_mask[:, None]
    weight = gates.reshape(-1)[row_ids] * live_mask
    quarter = FF // N_DP
    gate_up = gate_up_w.astype(jnp.float32).reshape(2, N_DP, quarter, D)
    down_matrix = down_w.astype(jnp.float32).reshape(N_DP, quarter, D)
    highest = lax.Precision.HIGHEST
    mixed_pre = jnp.einsum("rd,jqfd->rjqf", inputs.astype(jnp.float32), gate_up, precision=highest)
    gate_pre = mixed_pre[:, 0]
    up_part = mixed_pre[:, 1]
    sigmoid_gate = jax.nn.sigmoid(gate_pre)
    active = gate_pre * sigmoid_gate
    hidden = (active * up_part).astype(jnp.bfloat16)
    output_part = jnp.einsum("rqf,qfd->qrd", hidden.astype(jnp.float32), down_matrix, precision=highest)
    gate_part = jnp.sum(output_part * upstream.astype(jnp.float32)[None], axis=2).astype(jnp.bfloat16)
    row_dg = jnp.sum(gate_part.astype(jnp.float32), axis=0).astype(jnp.bfloat16)
    scaled = (weight.astype(jnp.float32)[:, None] * upstream.astype(jnp.float32)).astype(jnp.bfloat16)
    grad_hidden = jnp.einsum("rd,qfd->rqf", scaled.astype(jnp.float32), down_matrix, precision=highest)
    grad_gate = grad_hidden * up_part * sigmoid_gate * (1.0 + gate_pre * (1.0 - sigmoid_gate))
    grad_mixed = jnp.stack([grad_gate, grad_hidden * active], axis=1).astype(jnp.bfloat16)
    input_part = jnp.einsum("rjqf,jqfd->qrd", grad_mixed.astype(jnp.float32), gate_up, precision=highest)
    row_dx = jnp.sum(input_part.astype(jnp.bfloat16).astype(jnp.float32), axis=0).astype(jnp.bfloat16)
    weight_gu = jnp.einsum("rd,rjqf->jqfd", inputs.astype(jnp.float32), grad_mixed.astype(jnp.float32), precision=highest)
    weight_down = jnp.einsum("rqf,rd->qfd", hidden.astype(jnp.float32), scaled.astype(jnp.float32), precision=highest)
    return row_dx, row_dg, weight_gu.reshape(2, FF, D), weight_down.reshape(FF, D)


def reference(tokens, grad_out, routing, replica, gates, host_expert, w_gate_up, w_down):
    expert_ids = lax.broadcasted_iota(jnp.int32, (EXPERTS, N_EXPERT), 0)
    helper_ids = lax.broadcasted_iota(jnp.int32, (EXPERTS, N_EXPERT), 1)
    matches = host_expert[None, :] == expert_ids
    listed = jnp.sum(matches.astype(jnp.int32), axis=1)
    helper_of = jnp.sum(jnp.where(matches, helper_ids, 0), axis=1).astype(jnp.int32)
    flat_route = routing.reshape(-1).astype(jnp.int32)
    flat_copy = replica.reshape(-1).astype(jnp.int32)
    usable = (flat_copy == 0) | (listed[flat_route] > 0)
    labels = jnp.where(usable, flat_copy * EXPERTS + flat_route, 2 * EXPERTS).astype(jnp.int32)
    ordering = jnp.argsort(labels, stable=True).astype(jnp.int32)
    counts = jnp.bincount(labels, length=2 * EXPERTS + 1).astype(jnp.int32)
    starts = (jnp.cumsum(counts) - counts).astype(jnp.int32)
    capacity = N_DP * BLOCK
    padded = jnp.concatenate([ordering, jnp.zeros((capacity,), jnp.int32)])

    def segment(label_id):
        row_ids = lax.dynamic_slice_in_dim(padded, starts[label_id], capacity).astype(jnp.int32)
        live_rows = lax.broadcasted_iota(jnp.int32, (capacity,), 0) < counts[label_id]
        return row_ids, live_rows

    def accumulate(totals, row_ids, live_rows, row_dx, row_dg):
        grad_tok, grad_row = totals
        live_mask = live_rows.astype(jnp.float32)
        grad_tok = grad_tok.at[row_ids // TOPK].add(row_dx.astype(jnp.float32) * live_mask[:, None])
        grad_row = grad_row.at[row_ids].add(row_dg.astype(jnp.float32) * live_mask)
        return grad_tok, grad_row

    def helper_step(totals, expert):
        row_ids, live_rows = segment(EXPERTS + expert)
        row_dx, row_dg, weight_gu, weight_down = expert_pass(tokens, grad_out, gates, row_ids, live_rows, w_gate_up[expert], w_down[expert])
        totals = accumulate(totals, row_ids, live_rows, row_dx, row_dg)
        return totals, (weight_gu.astype(jnp.bfloat16), weight_down.astype(jnp.bfloat16))

    start_totals = (jnp.zeros((TOKENS, D), jnp.float32), jnp.zeros((TOKENS * TOPK,), jnp.float32))
    totals, helper_parts = lax.scan(helper_step, start_totals, host_expert.astype(jnp.int32))
    helper_gu, helper_down = helper_parts

    def owner_step(totals, expert):
        row_ids, live_rows = segment(expert)
        row_dx, row_dg, weight_gu, weight_down = expert_pass(tokens, grad_out, gates, row_ids, live_rows, w_gate_up[expert], w_down[expert])
        totals = accumulate(totals, row_ids, live_rows, row_dx, row_dg)
        present = (listed[expert] > 0).astype(jnp.float32)
        extra_gu = helper_gu[helper_of[expert]].astype(jnp.float32) * present
        extra_down = helper_down[helper_of[expert]].astype(jnp.float32) * present
        return totals, ((weight_gu + extra_gu).astype(jnp.bfloat16), (weight_down + extra_down).astype(jnp.bfloat16))

    totals, owner_parts = lax.scan(owner_step, totals, jnp.arange(EXPERTS, dtype=jnp.int32))
    grad_tok, grad_row = totals
    grad_w_gate_up, grad_w_down = owner_parts
    return grad_tok.astype(jnp.bfloat16), grad_row.reshape(TOKENS, TOPK), grad_w_gate_up, grad_w_down
```

```python
import jax
import jax.numpy as jnp
from jax import lax
from jax.sharding import PartitionSpec as P


def lookup(values_table, indices):
    matches = indices[..., None] == lax.broadcasted_iota(
        jnp.int32, indices.shape + values_table.shape, indices.ndim
    )
    return jnp.sum(jnp.where(matches, values_table, 0), axis=-1)


def placement(host_expert, owned_experts, devices):
    experts = owned_experts * devices
    matches = host_expert[None, :] == lax.broadcasted_iota(jnp.int32, (experts, devices), 0)
    helper_ids = lax.broadcasted_iota(jnp.int32, (experts, devices), 1)
    helper_of = jnp.sum(jnp.where(matches, helper_ids, 0), axis=1)
    listed = jnp.sum(matches.astype(jnp.int32), axis=1)
    return (helper_of, listed)


def targets(routing, replica, host_expert, owned_experts, devices, slot_rows, groups):
    helper_of, listed = placement(host_expert, owned_experts, devices)
    choices = routing.shape[0] // groups * routing.shape[1]
    usable = (replica == 0) | (lookup(listed, routing) > 0)
    device_to = jnp.where(replica == 0, routing // owned_experts, lookup(helper_of, routing))
    block_to = jnp.where(replica == 0, routing % owned_experts, owned_experts)
    labels = (routing * 2 + replica).reshape(groups, choices)
    earlier = lax.broadcasted_iota(jnp.int32, (choices, choices), 1) < lax.broadcasted_iota(
        jnp.int32, (choices, choices), 0
    )
    matching = (labels[:, :, None] == labels[:, None, :]) & earlier[None]
    ranking = jnp.sum(matching.astype(jnp.int32), axis=2).reshape(routing.shape)
    group_ids = lax.broadcasted_iota(jnp.int32, (groups, choices), 0).reshape(routing.shape)
    position = ((block_to * groups + group_ids) * devices + device_to) * slot_rows + ranking
    return jnp.where(usable, position, -1)


def selector(position, total_slots):
    matches = position[None, :, :] == lax.broadcasted_iota(
        jnp.int32, (total_slots,) + position.shape, 0
    )
    picker = jnp.sum(matches.astype(jnp.float32), axis=2).astype(jnp.bfloat16)
    return (matches, picker)


def fill_rows(matches, picker, tokens, grad_out, gates):
    row_x = jnp.dot(picker, tokens, preferred_element_type=jnp.float32).astype(jnp.bfloat16)
    row_dy = jnp.dot(picker, grad_out, preferred_element_type=jnp.float32).astype(jnp.bfloat16)
    row_gate = jnp.sum(
        jnp.where(matches, gates[None].astype(jnp.float32), 0.0), axis=(1, 2)
    ).astype(jnp.bfloat16)
    return (row_x, row_dy, row_gate)


def expert_block(inputs, upstream, weight, gate_up, down_matrix):
    mixed = jnp.einsum("rd,jfd->jrf", inputs, gate_up, preferred_element_type=jnp.float32)
    gate_pre = mixed[0]
    up_part = mixed[1]
    sigmoid_gate = jax.nn.sigmoid(gate_pre)
    active = gate_pre * sigmoid_gate
    hidden = (active * up_part).astype(jnp.bfloat16)
    output_part = jnp.einsum("rf,fd->rd", hidden, down_matrix, preferred_element_type=jnp.float32)
    gate_part = jnp.sum(output_part * upstream.astype(jnp.float32), axis=1)
    scaled = (weight.astype(jnp.float32)[:, None] * upstream.astype(jnp.float32)).astype(
        jnp.bfloat16
    )
    grad_hidden = jnp.einsum("rd,fd->rf", scaled, down_matrix, preferred_element_type=jnp.float32)
    grad_gate = grad_hidden * up_part * sigmoid_gate * (1.0 + gate_pre * (1.0 - sigmoid_gate))
    grad_mixed = jnp.stack([grad_gate, grad_hidden * active], axis=0).astype(jnp.bfloat16)
    input_part = jnp.einsum("jrf,jfd->rd", grad_mixed, gate_up, preferred_element_type=jnp.float32)
    weight_gu = jnp.einsum("jrf,rd->jfd", grad_mixed, inputs, preferred_element_type=jnp.float32)
    weight_down = jnp.einsum("rf,rd->fd", hidden, scaled, preferred_element_type=jnp.float32)
    return (input_part, gate_part, weight_gu, weight_down)


def shards(tokens, grad_out, routing, replica, gates, host_expert, w_gate_up, w_down):
    devices = lax.axis_size("expert")
    device_id = lax.axis_index("expert")
    token_rows, features = tokens.shape
    owned_experts = w_gate_up.shape[0]
    quarter = w_down.shape[1]
    topk_width = routing.shape[1]
    slot_rows = token_rows * topk_width // (owned_experts * devices)
    blocks = owned_experts + 1
    lane_rows = devices * slot_rows
    piece_rows = quarter // devices
    home_slots = targets(routing, replica, host_expert, owned_experts, devices, slot_rows, 1)
    home_matches, home_picker = selector(home_slots, blocks * lane_rows)
    row_x, row_dy, row_gate = fill_rows(home_matches, home_picker, tokens, grad_out, gates)
    sent_x, sent_dy, sent_gate = (
        lax.all_to_all(
            row_x.reshape(blocks, lane_rows, features),
            "expert",
            split_axis=1,
            concat_axis=1,
            tiled=True,
        ),
        lax.all_to_all(
            row_dy.reshape(blocks, lane_rows, features),
            "expert",
            split_axis=1,
            concat_axis=1,
            tiled=True,
        ),
        lax.all_to_all(
            row_gate.reshape(blocks, lane_rows), "expert", split_axis=1, concat_axis=1, tiled=True
        ),
    )
    block_x, block_dy, block_gate = (
        lax.all_gather(sent_x, "dp", axis=1, tiled=True),
        lax.all_gather(sent_dy, "dp", axis=1, tiled=True),
        lax.all_gather(sent_gate, "dp", axis=1, tiled=True),
    )
    owner_of_helper = host_expert // owned_experts
    owns_copy = owner_of_helper == device_id
    copied_local = jnp.sum(jnp.where(owns_copy, host_expert % owned_experts, 0))
    helper_ids = lax.broadcasted_iota(jnp.int32, (devices, devices), 1)
    owner_ids = lax.broadcasted_iota(jnp.int32, (devices, devices), 0)
    helper_of_owner = jnp.sum(
        jnp.where(owner_of_helper[None, :] == owner_ids, helper_ids, 0), axis=1
    )
    source_gu = lax.dynamic_index_in_dim(w_gate_up, copied_local, 0, keepdims=False)
    source_down = lax.dynamic_index_in_dim(w_down, copied_local, 0, keepdims=False)
    spread_gu, spread_down = (
        lax.all_to_all(
            source_gu.reshape(2, devices, piece_rows, features),
            "expert",
            split_axis=1,
            concat_axis=1,
            tiled=True,
        ),
        lax.all_to_all(
            source_down.reshape(1, devices, piece_rows, features),
            "expert",
            split_axis=1,
            concat_axis=1,
            tiled=True,
        ),
    )
    spread_gu = jnp.take(spread_gu, owner_of_helper, axis=1)
    spread_down = jnp.take(spread_down, owner_of_helper, axis=1)
    hosted_gu, hosted_down = (
        lax.all_to_all(spread_gu, "expert", split_axis=1, concat_axis=1, tiled=True),
        lax.all_to_all(spread_down, "expert", split_axis=1, concat_axis=1, tiled=True),
    )
    hosted_gu = hosted_gu.reshape(2, quarter, features)
    hosted_down = hosted_down.reshape(quarter, features)
    input_parts = []
    gate_parts = []
    owner_gu = []
    owner_down = []
    for block in range(blocks):
        if block < owned_experts:
            gate_up = w_gate_up[block]
            down_matrix = w_down[block]
        else:
            gate_up = hosted_gu
            down_matrix = hosted_down
        input_part, gate_part, weight_gu, weight_down = expert_block(
            block_x[block], block_dy[block], block_gate[block], gate_up, down_matrix
        )
        input_parts.append(input_part.astype(jnp.bfloat16))
        gate_parts.append(gate_part.astype(jnp.bfloat16))
        owner_gu.append(weight_gu)
        owner_down.append(weight_down)
    helper_gu = owner_gu[owned_experts].astype(jnp.bfloat16)
    helper_down = owner_down[owned_experts].astype(jnp.bfloat16)
    back_gu, back_down = (
        lax.all_to_all(
            helper_gu.reshape(2, devices, piece_rows, features),
            "expert",
            split_axis=1,
            concat_axis=1,
            tiled=True,
        ),
        lax.all_to_all(
            helper_down.reshape(1, devices, piece_rows, features),
            "expert",
            split_axis=1,
            concat_axis=1,
            tiled=True,
        ),
    )
    back_gu = jnp.take(back_gu, helper_of_owner, axis=1)
    back_down = jnp.take(back_down, helper_of_owner, axis=1)
    extra_gu, extra_down = (
        lax.all_to_all(back_gu, "expert", split_axis=1, concat_axis=1, tiled=True),
        lax.all_to_all(back_down, "expert", split_axis=1, concat_axis=1, tiled=True),
    )
    extra_gu = extra_gu.reshape(2, quarter, features).astype(jnp.float32)
    extra_down = extra_down.reshape(quarter, features).astype(jnp.float32)
    stacked_dx = jnp.stack(input_parts, axis=0)
    stacked_dg = jnp.stack(gate_parts, axis=0)
    summed_dx, summed_dg = (
        lax.psum_scatter(stacked_dx, "dp", scatter_dimension=1, tiled=True).astype(jnp.float32),
        lax.psum_scatter(stacked_dg, "dp", scatter_dimension=1, tiled=True).astype(jnp.float32),
    )
    row_dx = summed_dx.astype(jnp.bfloat16)
    row_dg = summed_dg.astype(jnp.bfloat16)
    home_dx, home_dg = (
        lax.all_to_all(row_dx, "expert", split_axis=1, concat_axis=1, tiled=True),
        lax.all_to_all(row_dg, "expert", split_axis=1, concat_axis=1, tiled=True),
    )
    home_dx = home_dx.reshape(blocks * lane_rows, features)
    home_dg = home_dg.reshape(blocks * lane_rows).astype(jnp.float32)
    grad_tokens = jnp.einsum(
        "st,sd->td", home_picker, home_dx, preferred_element_type=jnp.float32
    ).astype(jnp.bfloat16)
    grad_gates = jnp.sum(jnp.where(home_matches, home_dg[:, None, None], 0.0), axis=0)
    grad_gu = []
    grad_down = []
    for block in range(owned_experts):
        present = (copied_local == block).astype(jnp.float32)
        grad_gu.append((owner_gu[block] + present * extra_gu).astype(jnp.bfloat16))
        grad_down.append((owner_down[block] + present * extra_down).astype(jnp.bfloat16))
    return (grad_tokens, grad_gates, jnp.stack(grad_gu, axis=0), jnp.stack(grad_down, axis=0))


def chosen_gates(routing, replica, gates, host_expert, experts):
    listed = jnp.any(routing[:, :, None] == host_expert[None, None, :], axis=2)
    usable = (replica == 0) | listed
    picks = usable[:, :, None] & (
        routing[:, :, None] == lax.broadcasted_iota(jnp.int32, routing.shape + (experts,), 2)
    )
    weights = jnp.sum(jnp.where(picks, gates.astype(jnp.float32)[:, :, None], 0.0), axis=1)
    return (picks, weights)


def gathered_shards(
    tokens, grad_out, routing, replica, gates, host_expert, w_gate_up, w_down
):
    devices = lax.axis_size("expert")
    device_id = lax.axis_index("expert")
    rows, features = tokens.shape
    owned = w_gate_up.shape[0]
    experts = owned * devices
    lanes = (experts + 127) // 128 * 128
    picks, weights = chosen_gates(routing, replica, gates, host_expert, experts)
    side = jnp.pad(weights.astype(jnp.bfloat16), ((0, 0), (0, lanes - experts)))
    payload = jnp.concatenate([tokens, grad_out, side], axis=1)
    payload = lax.all_gather(payload, ("dp", "expert"), axis=0, tiled=True)
    every_x = payload[:, :features]
    every_dy = payload[:, features : 2 * features]
    own_gates = lax.dynamic_slice_in_dim(
        payload[:, 2 * features : 2 * features + experts], device_id * owned, owned, axis=1
    ).astype(jnp.float32)
    mixed = jnp.einsum("td,ejfd->jtef", every_x, w_gate_up, preferred_element_type=jnp.float32)
    raw_hidden = jnp.einsum("td,efd->tef", every_dy, w_down, preferred_element_type=jnp.float32)
    gate_pre = mixed[0]
    up_part = mixed[1]
    sigmoid_gate = jax.nn.sigmoid(gate_pre)
    active = gate_pre * sigmoid_gate
    hidden = (active * up_part).astype(jnp.bfloat16).astype(jnp.float32)
    gate_part = jnp.sum(hidden * raw_hidden, axis=2)
    weighted = (hidden * own_gates[:, :, None]).astype(jnp.bfloat16)
    grad_hidden = raw_hidden * own_gates[:, :, None]
    grad_gate = grad_hidden * up_part * sigmoid_gate * (1.0 + gate_pre * (1.0 - sigmoid_gate))
    grad_mixed = jnp.stack([grad_gate, grad_hidden * active], axis=0).astype(jnp.bfloat16)
    input_part = jnp.einsum(
        "jtef,ejfd->td", grad_mixed, w_gate_up, preferred_element_type=jnp.float32
    ).astype(jnp.bfloat16)
    slots = lax.broadcasted_iota(jnp.int32, (owned, lanes), 1)
    starts = device_id * owned + lax.broadcasted_iota(jnp.int32, (owned, lanes), 0)
    gate_side = jnp.sum(
        jnp.where((slots == starts)[None], gate_part[:, :, None], 0.0), axis=1
    ).astype(jnp.bfloat16)
    partial = jnp.concatenate([input_part, gate_side], axis=1)
    summed = lax.psum_scatter(partial, ("dp", "expert"), scatter_dimension=0, tiled=True)
    grad_gu = jnp.einsum(
        "jtef,td->ejfd", grad_mixed, every_x, preferred_element_type=jnp.float32
    ).astype(jnp.bfloat16)
    grad_down = jnp.einsum(
        "tef,td->efd", weighted, every_dy, preferred_element_type=jnp.float32
    ).astype(jnp.bfloat16)
    grad_tokens = summed[:, :features]
    sums = summed[:, features : features + experts].astype(jnp.float32)
    grad_gates = jnp.sum(jnp.where(picks, sums[:, None, :], 0.0), axis=2)
    return (grad_tokens, grad_gates, grad_gu, grad_down)


def serve(tokens, grad_out, routing, replica, gates, host_expert, w_gate_up, w_down):
    body = gathered_shards if routing.shape[1] >= lax.axis_size("expert") else shards
    return body(tokens, grad_out, routing, replica, gates, host_expert, w_gate_up, w_down)


def solution(mesh):
    in_specs = (
        P(("dp", "expert"), None),
        P(("dp", "expert"), None),
        P(("dp", "expert"), None),
        P(("dp", "expert"), None),
        P(("dp", "expert"), None),
        P(),
        P("expert", None, "dp", None),
        P("expert", "dp", None),
    )
    out_specs = (
        P(("dp", "expert"), None),
        P(("dp", "expert"), None),
        P("expert", None, "dp", None),
        P("expert", "dp", None),
    )
    return jax.shard_map(serve, mesh=mesh, in_specs=in_specs, out_specs=out_specs, check_vma=False)
```

```python
import functools

import jax
import jax.numpy as jnp
from jax import lax
from jax.experimental import pallas as pl
from jax.experimental.pallas import tpu as pltpu
from jax.sharding import PartitionSpec as P

MESH = pl.DeviceIdType.MESH


def lookup(values_table, indices):
    matches = indices[..., None] == lax.broadcasted_iota(
        jnp.int32, indices.shape + values_table.shape, indices.ndim
    )
    return jnp.sum(jnp.where(matches, values_table, 0), axis=-1)


def placement(host_expert, owned_experts, devices):
    experts = owned_experts * devices
    matches = host_expert[None, :] == lax.broadcasted_iota(jnp.int32, (experts, devices), 0)
    helper_ids = lax.broadcasted_iota(jnp.int32, (experts, devices), 1)
    helper_of = jnp.sum(jnp.where(matches, helper_ids, 0), axis=1)
    listed = jnp.sum(matches.astype(jnp.int32), axis=1)
    return (helper_of, listed)


def targets(routing, replica, host_expert, owned_experts, devices, slot_rows, groups):
    helper_of, listed = placement(host_expert, owned_experts, devices)
    choices = routing.shape[0] // groups * routing.shape[1]
    usable = (replica == 0) | (lookup(listed, routing) > 0)
    device_to = jnp.where(replica == 0, routing // owned_experts, lookup(helper_of, routing))
    block_to = jnp.where(replica == 0, routing % owned_experts, owned_experts)
    labels = (routing * 2 + replica).reshape(groups, choices)
    earlier = lax.broadcasted_iota(jnp.int32, (choices, choices), 1) < lax.broadcasted_iota(
        jnp.int32, (choices, choices), 0
    )
    matching = (labels[:, :, None] == labels[:, None, :]) & earlier[None]
    ranking = jnp.sum(matching.astype(jnp.int32), axis=2).reshape(routing.shape)
    group_ids = lax.broadcasted_iota(jnp.int32, (groups, choices), 0).reshape(routing.shape)
    position = ((block_to * groups + group_ids) * devices + device_to) * slot_rows + ranking
    return jnp.where(usable, position, -1)


def selector(position, total_slots):
    matches = position[None, :, :] == lax.broadcasted_iota(
        jnp.int32, (total_slots,) + position.shape, 0
    )
    picker = jnp.sum(matches.astype(jnp.float32), axis=2).astype(jnp.bfloat16)
    return (matches, picker)


def fill_rows(matches, picker, tokens, grad_out, gates):
    row_x = jnp.dot(picker, tokens, preferred_element_type=jnp.float32).astype(jnp.bfloat16)
    row_dy = jnp.dot(picker, grad_out, preferred_element_type=jnp.float32).astype(jnp.bfloat16)
    row_gate = jnp.sum(
        jnp.where(matches, gates[None].astype(jnp.float32), 0.0), axis=(1, 2)
    ).astype(jnp.bfloat16)
    return (row_x, row_dy, row_gate)


def expert_block(inputs, upstream, weight, gate_up, down_matrix):
    mixed = jnp.einsum("rd,jfd->jrf", inputs, gate_up, preferred_element_type=jnp.float32)
    gate_pre = mixed[0]
    up_part = mixed[1]
    sigmoid_gate = jax.nn.sigmoid(gate_pre)
    active = gate_pre * sigmoid_gate
    hidden = (active * up_part).astype(jnp.bfloat16)
    output_part = jnp.einsum("rf,fd->rd", hidden, down_matrix, preferred_element_type=jnp.float32)
    gate_part = jnp.sum(output_part * upstream.astype(jnp.float32), axis=1)
    scaled = (weight.astype(jnp.float32)[:, None] * upstream.astype(jnp.float32)).astype(
        jnp.bfloat16
    )
    grad_hidden = jnp.einsum("rd,fd->rf", scaled, down_matrix, preferred_element_type=jnp.float32)
    grad_gate = grad_hidden * up_part * sigmoid_gate * (1.0 + gate_pre * (1.0 - sigmoid_gate))
    grad_mixed = jnp.stack([grad_gate, grad_hidden * active], axis=0).astype(jnp.bfloat16)
    input_part = jnp.einsum("jrf,jfd->rd", grad_mixed, gate_up, preferred_element_type=jnp.float32)
    weight_gu = jnp.einsum("jrf,rd->jfd", grad_mixed, inputs, preferred_element_type=jnp.float32)
    weight_down = jnp.einsum("rf,rd->fd", hidden, scaled, preferred_element_type=jnp.float32)
    return (input_part, gate_part, weight_gu, weight_down)


def shards(tokens, grad_out, routing, replica, gates, host_expert, w_gate_up, w_down):
    devices = lax.axis_size("expert")
    device_id = lax.axis_index("expert")
    token_rows, features = tokens.shape
    owned_experts = w_gate_up.shape[0]
    quarter = w_down.shape[1]
    topk_width = routing.shape[1]
    slot_rows = token_rows * topk_width // (owned_experts * devices)
    blocks = owned_experts + 1
    lane_rows = devices * slot_rows
    piece_rows = quarter // devices
    home_slots = targets(routing, replica, host_expert, owned_experts, devices, slot_rows, 1)
    home_matches, home_picker = selector(home_slots, blocks * lane_rows)
    row_x, row_dy, row_gate = fill_rows(home_matches, home_picker, tokens, grad_out, gates)
    sent_x, sent_dy, sent_gate = (
        lax.all_to_all(
            row_x.reshape(blocks, lane_rows, features),
            "expert",
            split_axis=1,
            concat_axis=1,
            tiled=True,
        ),
        lax.all_to_all(
            row_dy.reshape(blocks, lane_rows, features),
            "expert",
            split_axis=1,
            concat_axis=1,
            tiled=True,
        ),
        lax.all_to_all(
            row_gate.reshape(blocks, lane_rows), "expert", split_axis=1, concat_axis=1, tiled=True
        ),
    )
    block_x, block_dy, block_gate = (
        lax.all_gather(sent_x, "dp", axis=1, tiled=True),
        lax.all_gather(sent_dy, "dp", axis=1, tiled=True),
        lax.all_gather(sent_gate, "dp", axis=1, tiled=True),
    )
    owner_of_helper = host_expert // owned_experts
    owns_copy = owner_of_helper == device_id
    copied_local = jnp.sum(jnp.where(owns_copy, host_expert % owned_experts, 0))
    helper_ids = lax.broadcasted_iota(jnp.int32, (devices, devices), 1)
    owner_ids = lax.broadcasted_iota(jnp.int32, (devices, devices), 0)
    helper_of_owner = jnp.sum(
        jnp.where(owner_of_helper[None, :] == owner_ids, helper_ids, 0), axis=1
    )
    source_gu = lax.dynamic_index_in_dim(w_gate_up, copied_local, 0, keepdims=False)
    source_down = lax.dynamic_index_in_dim(w_down, copied_local, 0, keepdims=False)
    spread_gu, spread_down = (
        lax.all_to_all(
            source_gu.reshape(2, devices, piece_rows, features),
            "expert",
            split_axis=1,
            concat_axis=1,
            tiled=True,
        ),
        lax.all_to_all(
            source_down.reshape(1, devices, piece_rows, features),
            "expert",
            split_axis=1,
            concat_axis=1,
            tiled=True,
        ),
    )
    spread_gu = jnp.take(spread_gu, owner_of_helper, axis=1)
    spread_down = jnp.take(spread_down, owner_of_helper, axis=1)
    hosted_gu, hosted_down = (
        lax.all_to_all(spread_gu, "expert", split_axis=1, concat_axis=1, tiled=True),
        lax.all_to_all(spread_down, "expert", split_axis=1, concat_axis=1, tiled=True),
    )
    hosted_gu = hosted_gu.reshape(2, quarter, features)
    hosted_down = hosted_down.reshape(quarter, features)
    input_parts = []
    gate_parts = []
    owner_gu = []
    owner_down = []
    for block in range(blocks):
        if block < owned_experts:
            gate_up = w_gate_up[block]
            down_matrix = w_down[block]
        else:
            gate_up = hosted_gu
            down_matrix = hosted_down
        input_part, gate_part, weight_gu, weight_down = expert_block(
            block_x[block], block_dy[block], block_gate[block], gate_up, down_matrix
        )
        input_parts.append(input_part.astype(jnp.bfloat16))
        gate_parts.append(gate_part.astype(jnp.bfloat16))
        owner_gu.append(weight_gu)
        owner_down.append(weight_down)
    helper_gu = owner_gu[owned_experts].astype(jnp.bfloat16)
    helper_down = owner_down[owned_experts].astype(jnp.bfloat16)
    back_gu, back_down = (
        lax.all_to_all(
            helper_gu.reshape(2, devices, piece_rows, features),
            "expert",
            split_axis=1,
            concat_axis=1,
            tiled=True,
        ),
        lax.all_to_all(
            helper_down.reshape(1, devices, piece_rows, features),
            "expert",
            split_axis=1,
            concat_axis=1,
            tiled=True,
        ),
    )
    back_gu = jnp.take(back_gu, helper_of_owner, axis=1)
    back_down = jnp.take(back_down, helper_of_owner, axis=1)
    extra_gu, extra_down = (
        lax.all_to_all(back_gu, "expert", split_axis=1, concat_axis=1, tiled=True),
        lax.all_to_all(back_down, "expert", split_axis=1, concat_axis=1, tiled=True),
    )
    extra_gu = extra_gu.reshape(2, quarter, features).astype(jnp.float32)
    extra_down = extra_down.reshape(quarter, features).astype(jnp.float32)
    stacked_dx = jnp.stack(input_parts, axis=0)
    stacked_dg = jnp.stack(gate_parts, axis=0)
    summed_dx, summed_dg = (
        lax.psum_scatter(stacked_dx, "dp", scatter_dimension=1, tiled=True).astype(jnp.float32),
        lax.psum_scatter(stacked_dg, "dp", scatter_dimension=1, tiled=True).astype(jnp.float32),
    )
    row_dx = summed_dx.astype(jnp.bfloat16)
    row_dg = summed_dg.astype(jnp.bfloat16)
    home_dx, home_dg = (
        lax.all_to_all(row_dx, "expert", split_axis=1, concat_axis=1, tiled=True),
        lax.all_to_all(row_dg, "expert", split_axis=1, concat_axis=1, tiled=True),
    )
    home_dx = home_dx.reshape(blocks * lane_rows, features)
    home_dg = home_dg.reshape(blocks * lane_rows).astype(jnp.float32)
    grad_tokens = jnp.einsum(
        "st,sd->td", home_picker, home_dx, preferred_element_type=jnp.float32
    ).astype(jnp.bfloat16)
    grad_gates = jnp.sum(jnp.where(home_matches, home_dg[:, None, None], 0.0), axis=0)
    grad_gu = []
    grad_down = []
    for block in range(owned_experts):
        present = (copied_local == block).astype(jnp.float32)
        grad_gu.append((owner_gu[block] + present * extra_gu).astype(jnp.bfloat16))
        grad_down.append((owner_down[block] + present * extra_down).astype(jnp.bfloat16))
    return (grad_tokens, grad_gates, jnp.stack(grad_gu, axis=0), jnp.stack(grad_down, axis=0))


def chosen_gates(routing, replica, gates, host_expert, experts):
    listed = jnp.any(routing[:, :, None] == host_expert[None, None, :], axis=2)
    usable = (replica == 0) | listed
    picks = usable[:, :, None] & (
        routing[:, :, None] == lax.broadcasted_iota(jnp.int32, routing.shape + (experts,), 2)
    )
    weights = jnp.sum(jnp.where(picks, gates.astype(jnp.float32)[:, :, None], 0.0), axis=1)
    return (picks, weights)


def greet(partners):
    barrier = pltpu.get_barrier_semaphore()
    for condition, device in partners:

        @pl.when(condition)
        def _():
            pl.semaphore_signal(barrier, inc=1, device_id=device, device_id_type=MESH)

    pl.semaphore_wait(barrier, sum(condition.astype(jnp.int32) for condition, _ in partners))


def place(depth):
    dp = lax.axis_index("dp")
    expert = lax.axis_index("expert")
    height, core = expert // 2, expert % 2
    row, column = dp // 2, dp % 2
    across = row * 2 + 1 - column
    along = (1 - row) * 2 + column
    diagonal = (1 - row) * 2 + 1 - column
    return dp, expert, height, core, across, along, diagonal


def gather_kernel(depth, source, out, sent, landed, local):
    dp, expert, height, core, across, along, diagonal = place(depth)
    half = source.shape[0] // 2
    partner = (dp, height * 2 + 1 - core)
    x_device = (across, expert)
    y_device = (along, expert)
    up_device = (dp, jnp.minimum(expert + 2, 2 * depth - 1))
    down_device = (dp, jnp.maximum(expert - 2, 0))
    has_up = height < depth - 1
    has_down = height > 0
    always = height >= 0
    greet(
        [
            (always, partner),
            (always, x_device),
            (always, y_device),
            (has_up, up_device),
            (has_down, down_device),
        ]
    )

    def slot_of(dp_from, height_from, core_from):
        return (dp_from * depth + height_from) * 2 + core_from

    def copy(slot, way, device, part=None, own=False):
        block = source if own else out.at[slot]
        into = out.at[slot]
        piece = 0
        if part is not None:
            block = block.at[pl.ds(part * half, half)]
            into = into.at[pl.ds(part * half, half)]
            piece = part
        return pltpu.make_async_remote_copy(
            src_ref=block,
            dst_ref=into,
            send_sem=sent.at[slot, way * 2 + piece],
            recv_sem=landed.at[slot, piece],
            device_id=device,
            device_id_type=MESH,
        )

    finish = []

    def send(condition, *args, **kwargs):
        finish.append((condition, args, kwargs))
        if condition is always:
            copy(*args, **kwargs).start()
        else:

            @pl.when(condition)
            def _():
                copy(*args, **kwargs).start()

    def arrive(condition, slot, part=None):
        if condition is always:
            copy(slot, 0, partner, part).wait_recv()
        else:

            @pl.when(condition)
            def _():
                copy(slot, 0, partner, part).wait_recv()

    def both(first, second):
        return first if second is always else jnp.logical_and(first, second)

    mine = slot_of(dp, height, core)
    send(has_up, mine, 3, up_device, own=True)
    send(has_down, mine, 4, down_device, own=True)
    send(always, mine, 1, x_device, own=True)
    send(always, mine, 2, y_device, own=True)
    send(always, mine, 0, partner, own=True)
    keep = pltpu.make_async_copy(source, out.at[mine], local)
    keep.start()
    steps = [[(always, height)]]
    for distance in range(1, depth):
        steps.append([(height >= distance, jnp.maximum(height - distance, 0))])
        steps[-1].append(
            (height + distance < depth, jnp.minimum(height + distance, depth - 1))
        )
    for index in range(depth + 2):
        if 0 < index < depth:
            for side, (condition, level) in enumerate(steps[index]):
                slot = slot_of(dp, level, core)
                arrive(condition, slot)
                if side == 0:
                    send(both(condition, has_up), slot, 3, up_device)
                else:
                    send(both(condition, has_down), slot, 4, down_device)
                send(condition, slot, 1, x_device)
                send(condition, slot, 2, y_device)
                send(condition, slot, 0, partner)
        if 0 <= index - 1 < depth:
            for condition, level in steps[index - 1]:
                slot = slot_of(across, level, core)
                arrive(condition, slot)
                send(condition, slot, 2, y_device, part=0)
                send(condition, slot, 0, partner)
                slot = slot_of(along, level, core)
                arrive(condition, slot)
                send(condition, slot, 1, x_device, part=1)
                send(condition, slot, 0, partner)
        if 0 <= index - 2 < depth:
            for condition, level in steps[index - 2]:
                slot = slot_of(diagonal, level, core)
                for part in range(2):
                    arrive(condition, slot, part)
                    send(condition, slot, 0, partner, part=part)
    keep.wait()
    for level in range(depth):
        for dp_from in (dp, across, along):
            arrive(always, slot_of(dp_from, level, 1 - core))
        for part in range(2):
            arrive(always, slot_of(diagonal, level, 1 - core), part)
    for condition, args, kwargs in finish:
        if condition is always:
            copy(*args, **kwargs).wait_send()
        else:

            @pl.when(condition)
            def _():
                copy(*args, **kwargs).wait_send()


def gather_rows(payload, dp_size, expert_size):
    rows, width = payload.shape
    depth = expert_size // 2
    slots = dp_size * expert_size
    out = pl.pallas_call(
        functools.partial(gather_kernel, depth),
        out_shape=jax.ShapeDtypeStruct((slots, rows, width), payload.dtype),
        in_specs=[pl.BlockSpec(memory_space=pl.ANY)],
        out_specs=pl.BlockSpec(memory_space=pl.ANY),
        scratch_shapes=[
            pltpu.SemaphoreType.DMA((slots, 10)),
            pltpu.SemaphoreType.DMA((slots, 2)),
            pltpu.SemaphoreType.DMA,
        ],
        compiler_params=pltpu.CompilerParams(collective_id=0, has_side_effects=True),
    )(payload)
    return out.reshape(slots * rows, width)


def scatter_kernel(
    depth, part_ref, out, paired, ready, crossed, column, risen, total, sems, landed
):
    dp, expert, height, core, across, along, diagonal = place(depth)
    others = (across, along, diagonal)
    partner = (dp, height * 2 + 1 - core)
    levels = [lax.rem(height + step, depth) for step in range(1, depth)] + [height]
    always = height >= 0
    greet(
        [(always, partner)]
        + [(always, (other, expert)) for other in others]
        + [(always, (dp, level * 2 + core)) for level in levels[:-1]]
    )

    def remote(block, into, index, device):
        return pltpu.make_async_remote_copy(
            src_ref=block,
            dst_ref=into,
            send_sem=sems.at[index],
            recv_sem=landed.at[index],
            device_id=device,
            device_id_type=MESH,
        )

    def pair_copy(step):
        return remote(part_ref.at[:, levels[step], 1 - core], paired.at[step], step, partner)

    def cross_copy(step, way):
        return remote(
            ready.at[step, way],
            crossed.at[step, way],
            depth + step * 3 + way,
            (others[way], expert),
        )

    def rise_copy(step):
        return remote(
            column.at[step], risen.at[step], 4 * depth + step, (dp, levels[step] * 2 + core)
        )

    for step in range(depth):
        pair_copy(step).start()
    for step in range(depth):
        pair_copy(step).wait_recv()
        for way in (2, 0, 1):
            ready[step, way] = (
                part_ref[others[way], levels[step], core].astype(jnp.float32)
                + paired[step, others[way]].astype(jnp.float32)
            ).astype(jnp.bfloat16)
            cross_copy(step, way).start()
    for step in range(depth):
        for way in range(3):
            cross_copy(step, way).wait_recv()
        summed = part_ref[dp, levels[step], core].astype(jnp.float32) + paired[
            step, dp
        ].astype(jnp.float32)
        for way in range(3):
            summed = summed + crossed[step, way].astype(jnp.float32)
        if step < depth - 1:
            column[step] = summed.astype(jnp.bfloat16)
            rise_copy(step).start()
        else:
            total[...] = summed
    for step in range(depth - 1):
        rise_copy(step).wait_recv()
        total[...] = total[...] + risen[step].astype(jnp.float32)
    out[...] = total[...].astype(jnp.bfloat16)
    for step in range(depth):
        pair_copy(step).wait_send()
        for way in range(3):
            cross_copy(step, way).wait_send()
        if step < depth - 1:
            rise_copy(step).wait_send()


def scatter_rows(partial, dp_size, expert_size):
    rows = partial.shape[0] // (dp_size * expert_size)
    width = partial.shape[1]
    depth = expert_size // 2
    block = (rows, width)
    return pl.pallas_call(
        functools.partial(scatter_kernel, depth),
        out_shape=jax.ShapeDtypeStruct(block, partial.dtype),
        in_specs=[pl.BlockSpec(memory_space=pltpu.VMEM)],
        out_specs=pl.BlockSpec(memory_space=pltpu.VMEM),
        scratch_shapes=[
            pltpu.VMEM((depth, dp_size) + block, jnp.bfloat16),
            pltpu.VMEM((depth, 3) + block, jnp.bfloat16),
            pltpu.VMEM((depth, 3) + block, jnp.bfloat16),
            pltpu.VMEM((depth,) + block, jnp.bfloat16),
            pltpu.VMEM((depth,) + block, jnp.bfloat16),
            pltpu.VMEM(block, jnp.float32),
            pltpu.SemaphoreType.DMA((5 * depth,)),
            pltpu.SemaphoreType.DMA((5 * depth,)),
        ],
        compiler_params=pltpu.CompilerParams(
            collective_id=1, has_side_effects=True, vmem_limit_bytes=48 << 20
        ),
    )(partial.reshape(dp_size, depth, 2, rows, width))


def gathered_shards(
    tokens, grad_out, routing, replica, gates, host_expert, w_gate_up, w_down
):
    devices = lax.axis_size("expert")
    device_id = lax.axis_index("expert")
    rows, features = tokens.shape
    owned = w_gate_up.shape[0]
    experts = owned * devices
    lanes = (experts + 127) // 128 * 128
    picks, weights = chosen_gates(routing, replica, gates, host_expert, experts)
    side = jnp.pad(weights.astype(jnp.bfloat16), ((0, 0), (0, lanes - experts)))
    payload = jnp.concatenate([tokens, grad_out, side], axis=1)
    dp_size = lax.axis_size("dp")
    payload = gather_rows(payload, dp_size, devices)
    every_x = payload[:, :features]
    every_dy = payload[:, features : 2 * features]
    own_gates = lax.dynamic_slice_in_dim(
        payload[:, 2 * features : 2 * features + experts], device_id * owned, owned, axis=1
    ).astype(jnp.float32)
    mixed = jnp.einsum("td,ejfd->jtef", every_x, w_gate_up, preferred_element_type=jnp.float32)
    raw_hidden = jnp.einsum("td,efd->tef", every_dy, w_down, preferred_element_type=jnp.float32)
    gate_pre = mixed[0]
    up_part = mixed[1]
    sigmoid_gate = jax.nn.sigmoid(gate_pre)
    active = gate_pre * sigmoid_gate
    hidden = (active * up_part).astype(jnp.bfloat16).astype(jnp.float32)
    gate_part = jnp.sum(hidden * raw_hidden, axis=2)
    weighted = (hidden * own_gates[:, :, None]).astype(jnp.bfloat16)
    grad_hidden = raw_hidden * own_gates[:, :, None]
    grad_gate = grad_hidden * up_part * sigmoid_gate * (1.0 + gate_pre * (1.0 - sigmoid_gate))
    grad_mixed = jnp.stack([grad_gate, grad_hidden * active], axis=0).astype(jnp.bfloat16)
    input_part = jnp.einsum(
        "jtef,ejfd->td", grad_mixed, w_gate_up, preferred_element_type=jnp.float32
    ).astype(jnp.bfloat16)
    slots = lax.broadcasted_iota(jnp.int32, (owned, lanes), 1)
    starts = device_id * owned + lax.broadcasted_iota(jnp.int32, (owned, lanes), 0)
    gate_side = jnp.sum(
        jnp.where((slots == starts)[None], gate_part[:, :, None], 0.0), axis=1
    ).astype(jnp.bfloat16)
    partial = jnp.concatenate([input_part, gate_side], axis=1)
    summed = scatter_rows(partial, dp_size, devices)
    grad_gu = jnp.einsum(
        "jtef,td->ejfd", grad_mixed, every_x, preferred_element_type=jnp.float32
    ).astype(jnp.bfloat16)
    grad_down = jnp.einsum(
        "tef,td->efd", weighted, every_dy, preferred_element_type=jnp.float32
    ).astype(jnp.bfloat16)
    grad_tokens = summed[:, :features]
    sums = summed[:, features : features + experts].astype(jnp.float32)
    grad_gates = jnp.sum(jnp.where(picks, sums[:, None, :], 0.0), axis=2)
    return (grad_tokens, grad_gates, grad_gu, grad_down)


def serve(tokens, grad_out, routing, replica, gates, host_expert, w_gate_up, w_down):
    squares = lax.axis_size("dp") == 4 and lax.axis_size("expert") % 2 == 0
    visits_all = routing.shape[1] >= lax.axis_size("expert")
    body = gathered_shards if squares and visits_all else shards
    return body(tokens, grad_out, routing, replica, gates, host_expert, w_gate_up, w_down)


def solution(mesh):
    in_specs = (
        P(("dp", "expert"), None),
        P(("dp", "expert"), None),
        P(("dp", "expert"), None),
        P(("dp", "expert"), None),
        P(("dp", "expert"), None),
        P(),
        P("expert", None, "dp", None),
        P("expert", "dp", None),
    )
    out_specs = (
        P(("dp", "expert"), None),
        P(("dp", "expert"), None),
        P("expert", None, "dp", None),
        P("expert", "dp", None),
    )
    return jax.shard_map(serve, mesh=mesh, in_specs=in_specs, out_specs=out_specs, check_vma=False)
```

```python
import functools

import jax
import jax.numpy as jnp
from jax import lax
from jax.experimental import pallas as pl
from jax.experimental.pallas import tpu as pltpu
from jax.sharding import PartitionSpec as P

MESH = pl.DeviceIdType.MESH


def lookup(values_table, indices):
    matches = indices[..., None] == lax.broadcasted_iota(
        jnp.int32, indices.shape + values_table.shape, indices.ndim
    )
    return jnp.sum(jnp.where(matches, values_table, 0), axis=-1)


def placement(host_expert, owned_experts, devices):
    experts = owned_experts * devices
    matches = host_expert[None, :] == lax.broadcasted_iota(jnp.int32, (experts, devices), 0)
    helper_ids = lax.broadcasted_iota(jnp.int32, (experts, devices), 1)
    helper_of = jnp.sum(jnp.where(matches, helper_ids, 0), axis=1)
    listed = jnp.sum(matches.astype(jnp.int32), axis=1)
    return (helper_of, listed)


def targets(routing, replica, host_expert, owned_experts, devices, slot_rows, groups):
    helper_of, listed = placement(host_expert, owned_experts, devices)
    choices = routing.shape[0] // groups * routing.shape[1]
    usable = (replica == 0) | (lookup(listed, routing) > 0)
    device_to = jnp.where(replica == 0, routing // owned_experts, lookup(helper_of, routing))
    block_to = jnp.where(replica == 0, routing % owned_experts, owned_experts)
    labels = (routing * 2 + replica).reshape(groups, choices)
    earlier = lax.broadcasted_iota(jnp.int32, (choices, choices), 1) < lax.broadcasted_iota(
        jnp.int32, (choices, choices), 0
    )
    matching = (labels[:, :, None] == labels[:, None, :]) & earlier[None]
    ranking = jnp.sum(matching.astype(jnp.int32), axis=2).reshape(routing.shape)
    group_ids = lax.broadcasted_iota(jnp.int32, (groups, choices), 0).reshape(routing.shape)
    position = ((block_to * groups + group_ids) * devices + device_to) * slot_rows + ranking
    return jnp.where(usable, position, -1)


def selector(position, total_slots):
    matches = position[None, :, :] == lax.broadcasted_iota(
        jnp.int32, (total_slots,) + position.shape, 0
    )
    picker = jnp.sum(matches.astype(jnp.float32), axis=2).astype(jnp.bfloat16)
    return (matches, picker)


def fill_rows(matches, picker, tokens, grad_out, gates):
    row_x = jnp.dot(picker, tokens, preferred_element_type=jnp.float32).astype(jnp.bfloat16)
    row_dy = jnp.dot(picker, grad_out, preferred_element_type=jnp.float32).astype(jnp.bfloat16)
    row_gate = jnp.sum(
        jnp.where(matches, gates[None].astype(jnp.float32), 0.0), axis=(1, 2)
    ).astype(jnp.bfloat16)
    return (row_x, row_dy, row_gate)


def expert_block(inputs, upstream, weight, gate_up, down_matrix):
    mixed = jnp.einsum("rd,jfd->jrf", inputs, gate_up, preferred_element_type=jnp.float32)
    gate_pre = mixed[0]
    up_part = mixed[1]
    sigmoid_gate = jax.nn.sigmoid(gate_pre)
    active = gate_pre * sigmoid_gate
    hidden = (active * up_part).astype(jnp.bfloat16)
    output_part = jnp.einsum("rf,fd->rd", hidden, down_matrix, preferred_element_type=jnp.float32)
    gate_part = jnp.sum(output_part * upstream.astype(jnp.float32), axis=1)
    scaled = (weight.astype(jnp.float32)[:, None] * upstream.astype(jnp.float32)).astype(
        jnp.bfloat16
    )
    grad_hidden = jnp.einsum("rd,fd->rf", scaled, down_matrix, preferred_element_type=jnp.float32)
    grad_gate = grad_hidden * up_part * sigmoid_gate * (1.0 + gate_pre * (1.0 - sigmoid_gate))
    grad_mixed = jnp.stack([grad_gate, grad_hidden * active], axis=0).astype(jnp.bfloat16)
    input_part = jnp.einsum("jrf,jfd->rd", grad_mixed, gate_up, preferred_element_type=jnp.float32)
    weight_gu = jnp.einsum("jrf,rd->jfd", grad_mixed, inputs, preferred_element_type=jnp.float32)
    weight_down = jnp.einsum("rf,rd->fd", hidden, scaled, preferred_element_type=jnp.float32)
    return (input_part, gate_part, weight_gu, weight_down)


def shards(tokens, grad_out, routing, replica, gates, host_expert, w_gate_up, w_down):
    devices = lax.axis_size("expert")
    device_id = lax.axis_index("expert")
    token_rows, features = tokens.shape
    owned_experts = w_gate_up.shape[0]
    quarter = w_down.shape[1]
    topk_width = routing.shape[1]
    slot_rows = token_rows * topk_width // (owned_experts * devices)
    blocks = owned_experts + 1
    lane_rows = devices * slot_rows
    piece_rows = quarter // devices
    home_slots = targets(routing, replica, host_expert, owned_experts, devices, slot_rows, 1)
    home_matches, home_picker = selector(home_slots, blocks * lane_rows)
    row_x, row_dy, row_gate = fill_rows(home_matches, home_picker, tokens, grad_out, gates)
    sent_x, sent_dy, sent_gate = (
        lax.all_to_all(
            row_x.reshape(blocks, lane_rows, features),
            "expert",
            split_axis=1,
            concat_axis=1,
            tiled=True,
        ),
        lax.all_to_all(
            row_dy.reshape(blocks, lane_rows, features),
            "expert",
            split_axis=1,
            concat_axis=1,
            tiled=True,
        ),
        lax.all_to_all(
            row_gate.reshape(blocks, lane_rows), "expert", split_axis=1, concat_axis=1, tiled=True
        ),
    )
    block_x, block_dy, block_gate = (
        lax.all_gather(sent_x, "dp", axis=1, tiled=True),
        lax.all_gather(sent_dy, "dp", axis=1, tiled=True),
        lax.all_gather(sent_gate, "dp", axis=1, tiled=True),
    )
    owner_of_helper = host_expert // owned_experts
    owns_copy = owner_of_helper == device_id
    copied_local = jnp.sum(jnp.where(owns_copy, host_expert % owned_experts, 0))
    helper_ids = lax.broadcasted_iota(jnp.int32, (devices, devices), 1)
    owner_ids = lax.broadcasted_iota(jnp.int32, (devices, devices), 0)
    helper_of_owner = jnp.sum(
        jnp.where(owner_of_helper[None, :] == owner_ids, helper_ids, 0), axis=1
    )
    source_gu = lax.dynamic_index_in_dim(w_gate_up, copied_local, 0, keepdims=False)
    source_down = lax.dynamic_index_in_dim(w_down, copied_local, 0, keepdims=False)
    spread_gu, spread_down = (
        lax.all_to_all(
            source_gu.reshape(2, devices, piece_rows, features),
            "expert",
            split_axis=1,
            concat_axis=1,
            tiled=True,
        ),
        lax.all_to_all(
            source_down.reshape(1, devices, piece_rows, features),
            "expert",
            split_axis=1,
            concat_axis=1,
            tiled=True,
        ),
    )
    spread_gu = jnp.take(spread_gu, owner_of_helper, axis=1)
    spread_down = jnp.take(spread_down, owner_of_helper, axis=1)
    hosted_gu, hosted_down = (
        lax.all_to_all(spread_gu, "expert", split_axis=1, concat_axis=1, tiled=True),
        lax.all_to_all(spread_down, "expert", split_axis=1, concat_axis=1, tiled=True),
    )
    hosted_gu = hosted_gu.reshape(2, quarter, features)
    hosted_down = hosted_down.reshape(quarter, features)
    input_parts = []
    gate_parts = []
    owner_gu = []
    owner_down = []
    for block in range(blocks):
        if block < owned_experts:
            gate_up = w_gate_up[block]
            down_matrix = w_down[block]
        else:
            gate_up = hosted_gu
            down_matrix = hosted_down
        input_part, gate_part, weight_gu, weight_down = expert_block(
            block_x[block], block_dy[block], block_gate[block], gate_up, down_matrix
        )
        input_parts.append(input_part.astype(jnp.bfloat16))
        gate_parts.append(gate_part.astype(jnp.bfloat16))
        owner_gu.append(weight_gu)
        owner_down.append(weight_down)
    helper_gu = owner_gu[owned_experts].astype(jnp.bfloat16)
    helper_down = owner_down[owned_experts].astype(jnp.bfloat16)
    back_gu, back_down = (
        lax.all_to_all(
            helper_gu.reshape(2, devices, piece_rows, features),
            "expert",
            split_axis=1,
            concat_axis=1,
            tiled=True,
        ),
        lax.all_to_all(
            helper_down.reshape(1, devices, piece_rows, features),
            "expert",
            split_axis=1,
            concat_axis=1,
            tiled=True,
        ),
    )
    back_gu = jnp.take(back_gu, helper_of_owner, axis=1)
    back_down = jnp.take(back_down, helper_of_owner, axis=1)
    extra_gu, extra_down = (
        lax.all_to_all(back_gu, "expert", split_axis=1, concat_axis=1, tiled=True),
        lax.all_to_all(back_down, "expert", split_axis=1, concat_axis=1, tiled=True),
    )
    extra_gu = extra_gu.reshape(2, quarter, features).astype(jnp.float32)
    extra_down = extra_down.reshape(quarter, features).astype(jnp.float32)
    stacked_dx = jnp.stack(input_parts, axis=0)
    stacked_dg = jnp.stack(gate_parts, axis=0)
    summed_dx, summed_dg = (
        lax.psum_scatter(stacked_dx, "dp", scatter_dimension=1, tiled=True).astype(jnp.float32),
        lax.psum_scatter(stacked_dg, "dp", scatter_dimension=1, tiled=True).astype(jnp.float32),
    )
    row_dx = summed_dx.astype(jnp.bfloat16)
    row_dg = summed_dg.astype(jnp.bfloat16)
    home_dx, home_dg = (
        lax.all_to_all(row_dx, "expert", split_axis=1, concat_axis=1, tiled=True),
        lax.all_to_all(row_dg, "expert", split_axis=1, concat_axis=1, tiled=True),
    )
    home_dx = home_dx.reshape(blocks * lane_rows, features)
    home_dg = home_dg.reshape(blocks * lane_rows).astype(jnp.float32)
    grad_tokens = jnp.einsum(
        "st,sd->td", home_picker, home_dx, preferred_element_type=jnp.float32
    ).astype(jnp.bfloat16)
    grad_gates = jnp.sum(jnp.where(home_matches, home_dg[:, None, None], 0.0), axis=0)
    grad_gu = []
    grad_down = []
    for block in range(owned_experts):
        present = (copied_local == block).astype(jnp.float32)
        grad_gu.append((owner_gu[block] + present * extra_gu).astype(jnp.bfloat16))
        grad_down.append((owner_down[block] + present * extra_down).astype(jnp.bfloat16))
    return (grad_tokens, grad_gates, jnp.stack(grad_gu, axis=0), jnp.stack(grad_down, axis=0))


def chosen_gates(routing, replica, gates, host_expert, experts):
    listed = jnp.any(routing[:, :, None] == host_expert[None, None, :], axis=2)
    usable = (replica == 0) | listed
    picks = usable[:, :, None] & (
        routing[:, :, None] == lax.broadcasted_iota(jnp.int32, routing.shape + (experts,), 2)
    )
    weights = jnp.sum(jnp.where(picks, gates.astype(jnp.float32)[:, :, None], 0.0), axis=1)
    return (picks, weights)


def greet(partners):
    barrier = pltpu.get_barrier_semaphore()
    for condition, device in partners:

        @pl.when(condition)
        def _():
            pl.semaphore_signal(barrier, inc=1, device_id=device, device_id_type=MESH)

    pl.semaphore_wait(barrier, sum(condition.astype(jnp.int32) for condition, _ in partners))


def fused_kernel(
    depth,
    features,
    source,
    gu_hbm,
    down_hbm,
    summed_ref,
    grad_gu_hbm,
    grad_down_hbm,
    rows_ref,
    gu_ref,
    down_ref,
    grad_gu_ref,
    grad_down_ref,
    mixed_ref,
    hidden_ref,
    part_ref,
    paired,
    ready,
    crossed,
    column_ref,
    risen,
    total,
    sent,
    landed,
    local,
    sums_sent,
    sums_landed,
):
    dp = lax.axis_index("dp")
    expert = lax.axis_index("expert")
    height, core = expert // 2, expert % 2
    row, column = dp // 2, dp % 2
    across = row * 2 + 1 - column
    along = (1 - row) * 2 + column
    diagonal = (1 - row) * 2 + 1 - column
    roles = (dp, across, along, diagonal)
    count, half = source.shape[0], source.shape[0] // 2
    owned = down_ref.shape[0]
    group_slots = 2 * depth
    group_rows = group_slots * count
    lanes = source.shape[1] - 2 * features
    partner = (dp, height * 2 + 1 - core)
    x_device = (across, expert)
    y_device = (along, expert)
    up_device = (dp, jnp.minimum(expert + 2, 2 * depth - 1))
    down_device = (dp, jnp.maximum(expert - 2, 0))
    has_up = height < depth - 1
    has_down = height > 0
    always = height >= 0
    levels = [lax.rem(height + step, depth) for step in range(1, depth)] + [height]
    loads = [
        pltpu.make_async_copy(gu_hbm, gu_ref, local.at[1]),
        pltpu.make_async_copy(down_hbm, down_ref, local.at[2]),
    ]
    for load in loads:
        load.start()
    greet(
        [
            (always, partner),
            (always, x_device),
            (always, y_device),
            (always, (diagonal, expert)),
        ]
        + [(always, (dp, level * 2 + core)) for level in levels[:-1]]
    )

    def slot_of(dp_from, height_from, core_from):
        return (dp_from * depth + height_from) * 2 + core_from

    def copy(slot, way, device, part=None, own=False):
        block = source if own else rows_ref.at[slot]
        into = rows_ref.at[slot]
        piece = 0
        if part is not None:
            block = block.at[pl.ds(part * half, half)]
            into = into.at[pl.ds(part * half, half)]
            piece = part
        return pltpu.make_async_remote_copy(
            src_ref=block,
            dst_ref=into,
            send_sem=sent.at[slot, way * 2 + piece],
            recv_sem=landed.at[slot, piece],
            device_id=device,
            device_id_type=MESH,
        )

    finish = []

    def guard(condition, action):
        if condition is always:
            action()
        else:
            pl.when(condition)(action)

    def send(condition, *args, **kwargs):
        finish.append((condition, args, kwargs))
        guard(condition, lambda: copy(*args, **kwargs).start())

    def arrive(condition, slot, part=None):
        guard(condition, lambda: copy(slot, 0, partner, part).wait_recv())

    def both(first, second):
        return first if second is always else jnp.logical_and(first, second)

    steps = [[(always, height)]]
    for distance in range(1, depth):
        steps.append([(height >= distance, jnp.maximum(height - distance, 0))])
        steps[-1].append(
            (height + distance < depth, jnp.minimum(height + distance, depth - 1))
        )

    def relay_column(index):
        for side, (condition, level) in enumerate(steps[index]):
            slot = slot_of(dp, level, core)
            arrive(condition, slot)
            if side == 0:
                send(both(condition, has_up), slot, 3, up_device)
            else:
                send(both(condition, has_down), slot, 4, down_device)
            send(condition, slot, 1, x_device)
            send(condition, slot, 2, y_device)
            send(condition, slot, 0, partner)

    def relay_sides(index):
        for condition, level in steps[index]:
            slot = slot_of(across, level, core)
            arrive(condition, slot)
            send(condition, slot, 2, y_device, part=0)
            send(condition, slot, 0, partner)
            slot = slot_of(along, level, core)
            arrive(condition, slot)
            send(condition, slot, 1, x_device, part=1)
            send(condition, slot, 0, partner)

    def relay_diagonal(index):
        for condition, level in steps[index]:
            slot = slot_of(diagonal, level, core)
            for part in range(2):
                arrive(condition, slot, part)
                send(condition, slot, 0, partner, part=part)

    def partner_rows(role):
        for level in range(depth):
            slot = slot_of(roles[role], level, 1 - core)
            if role == 3:
                arrive(always, slot, 0)
                arrive(always, slot, 1)
            else:
                arrive(always, slot)

    def remote(block, into, index, device):
        return pltpu.make_async_remote_copy(
            src_ref=block,
            dst_ref=into,
            send_sem=sums_sent.at[index],
            recv_sem=sums_landed.at[index],
            device_id=device,
            device_id_type=MESH,
        )

    def pair_copy(role):
        return remote(part_ref.at[roles[role], :, 1 - core], paired.at[role], role, partner)

    def cross_copy(step, way):
        return remote(
            ready.at[step, way],
            crossed.at[step, way],
            4 + step * 3 + way,
            (roles[way + 1], expert),
        )

    def rise_copy(step):
        return remote(
            column_ref.at[step],
            risen.at[step],
            4 + 3 * depth + step,
            (dp, levels[step] * 2 + core),
        )

    def group(role):
        return pl.ds(roles[role] * group_slots, group_slots)

    def rows_by_columns(a, b):
        return lax.dot_general(
            a, b, (((1,), (1,)), ((), ())), preferred_element_type=jnp.float32
        )

    def compute(role):
        inputs = rows_ref[group(role), :, :features].reshape(group_rows, features)
        upstream = rows_ref[group(role), :, features : 2 * features].reshape(
            group_rows, features
        )
        side = rows_ref[group(role), :, 2 * features :].reshape(group_rows, lanes)
        side = side.astype(jnp.float32)
        slots = lax.broadcasted_iota(jnp.int32, side.shape, 1)
        gate_side = jnp.zeros(side.shape, jnp.float32)
        for local_expert in range(owned):
            at_expert = slots == expert * owned + local_expert
            weight = jnp.sum(jnp.where(at_expert, side, 0.0), axis=1, keepdims=True)
            gate_pre = rows_by_columns(inputs, gu_ref[local_expert, 0])
            up_part = rows_by_columns(inputs, gu_ref[local_expert, 1])
            raw_hidden = rows_by_columns(upstream, down_ref[local_expert])
            sigmoid_gate = jax.nn.sigmoid(gate_pre)
            active = gate_pre * sigmoid_gate
            hidden = (active * up_part).astype(jnp.bfloat16).astype(jnp.float32)
            gate_part = jnp.sum(hidden * raw_hidden, axis=1, keepdims=True)
            gate_side = jnp.where(at_expert, gate_part, gate_side)
            grad_hidden = raw_hidden * weight
            grad_gate = (
                grad_hidden * up_part * sigmoid_gate * (1.0 + gate_pre * (1.0 - sigmoid_gate))
            )
            hidden_ref[local_expert, roles[role]] = (hidden * weight).astype(jnp.bfloat16)
            mixed_ref[2 * local_expert, roles[role]] = grad_gate.astype(jnp.bfloat16)
            mixed_ref[2 * local_expert + 1, roles[role]] = (grad_hidden * active).astype(
                jnp.bfloat16
            )
        dx = jnp.zeros((group_rows, features), jnp.float32)
        for index in range(2 * owned):
            dx = dx + jnp.dot(
                mixed_ref[index, roles[role]],
                gu_ref[index // 2, index % 2],
                preferred_element_type=jnp.float32,
            )
        shape = (depth, 2, count)
        part_ref[roles[role], :, :, :, :features] = dx.astype(jnp.bfloat16).reshape(
            shape + (features,)
        )
        part_ref[roles[role], :, :, :, features:] = gate_side.astype(jnp.bfloat16).reshape(
            shape + (lanes,)
        )
        pair_copy(role).start()

    def combine(role):
        pair_copy(role).wait_recv()
        if role > 0:
            for step in range(depth):
                ready[step, role - 1] = (
                    part_ref[roles[role], levels[step], core].astype(jnp.float32)
                    + paired[role, levels[step]].astype(jnp.float32)
                ).astype(jnp.bfloat16)
                cross_copy(step, role - 1).start()

    def columns_by_columns(a, b):
        return lax.dot_general(
            a, b, (((0,), (0,)), ((), ())), preferred_element_type=jnp.float32
        ).astype(jnp.bfloat16)

    total_rows = 4 * group_rows
    quarter = mixed_ref.shape[3]

    def down_grads():
        upstream = rows_ref[:, :, features : 2 * features].reshape(total_rows, features)
        for local_expert in range(owned):
            weighted = hidden_ref[local_expert].reshape(total_rows, quarter)
            grad_down_ref[local_expert] = columns_by_columns(weighted, upstream)
        pltpu.make_async_copy(grad_down_ref, grad_down_hbm, local.at[2]).start()

    def gu_grads():
        inputs = rows_ref[:, :, :features].reshape(total_rows, features)
        for index in range(2 * owned):
            grads = mixed_ref[index].reshape(total_rows, quarter)
            grad_gu_ref[index // 2, index % 2] = columns_by_columns(grads, inputs)
        pltpu.make_async_copy(grad_gu_ref, grad_gu_hbm, local.at[1]).start()

    mine = slot_of(dp, height, core)
    send(has_up, mine, 3, up_device, own=True)
    send(has_down, mine, 4, down_device, own=True)
    send(always, mine, 1, x_device, own=True)
    send(always, mine, 2, y_device, own=True)
    send(always, mine, 0, partner, own=True)
    keep = pltpu.make_async_copy(source, rows_ref.at[mine], local.at[0])
    keep.start()
    for index in range(1, depth):
        relay_column(index)
        relay_sides(index - 1)
    keep.wait()
    for load in loads:
        load.wait()
    partner_rows(0)
    compute(0)
    relay_sides(depth - 1)
    relay_diagonal(0)
    partner_rows(1)
    compute(1)
    for index in range(1, depth - 1):
        relay_diagonal(index)
    partner_rows(2)
    compute(2)
    combine(0)
    combine(1)
    relay_diagonal(depth - 1)
    partner_rows(3)
    compute(3)
    combine(2)
    down_grads()
    combine(3)
    gu_grads()
    for step in range(depth):
        for way in range(3):
            cross_copy(step, way).wait_recv()
        summed = part_ref[dp, levels[step], core].astype(jnp.float32) + paired[
            0, levels[step]
        ].astype(jnp.float32)
        for way in range(3):
            summed = summed + crossed[step, way].astype(jnp.float32)
        if step < depth - 1:
            column_ref[step] = summed.astype(jnp.bfloat16)
            rise_copy(step).start()
        else:
            total[...] = summed
    for step in range(depth - 1):
        rise_copy(step).wait_recv()
        total[...] = total[...] + risen[step].astype(jnp.float32)
    summed_ref[...] = total[...].astype(jnp.bfloat16)
    for condition, args, kwargs in finish:
        guard(condition, lambda args=args, kwargs=kwargs: copy(*args, **kwargs).wait_send())
    for role in range(4):
        pair_copy(role).wait_send()
    for step in range(depth):
        for way in range(3):
            cross_copy(step, way).wait_send()
        if step < depth - 1:
            rise_copy(step).wait_send()
    pltpu.make_async_copy(grad_down_ref, grad_down_hbm, local.at[2]).wait()
    pltpu.make_async_copy(grad_gu_ref, grad_gu_hbm, local.at[1]).wait()


def fused_layer(payload, w_gate_up, w_down, expert_size):
    count, width = payload.shape
    features = w_down.shape[2]
    owned, quarter = w_down.shape[:2]
    depth = expert_size // 2
    slots = 4 * expert_size
    sums = width - features
    block = (count, sums)
    group_rows = expert_size * count
    kind = jnp.bfloat16
    anywhere = pl.BlockSpec(memory_space=pl.ANY)
    return pl.pallas_call(
        functools.partial(fused_kernel, depth, features),
        out_shape=(
            jax.ShapeDtypeStruct(block, kind),
            jax.ShapeDtypeStruct(w_gate_up.shape, kind),
            jax.ShapeDtypeStruct(w_down.shape, kind),
        ),
        in_specs=[anywhere] * 3,
        out_specs=(pl.BlockSpec(memory_space=pltpu.VMEM), anywhere, anywhere),
        scratch_shapes=[
            pltpu.VMEM((slots, count, width), kind),
            pltpu.VMEM(w_gate_up.shape, kind),
            pltpu.VMEM(w_down.shape, kind),
            pltpu.VMEM(w_gate_up.shape, kind),
            pltpu.VMEM(w_down.shape, kind),
            pltpu.VMEM((2 * owned, 4, group_rows, quarter), kind),
            pltpu.VMEM((owned, 4, group_rows, quarter), kind),
            pltpu.VMEM((4, depth, 2) + block, kind),
            pltpu.VMEM((4, depth) + block, kind),
            pltpu.VMEM((depth, 3) + block, kind),
            pltpu.VMEM((depth, 3) + block, kind),
            pltpu.VMEM((depth,) + block, kind),
            pltpu.VMEM((depth,) + block, kind),
            pltpu.VMEM(block, jnp.float32),
            pltpu.SemaphoreType.DMA((slots, 10)),
            pltpu.SemaphoreType.DMA((slots, 2)),
            pltpu.SemaphoreType.DMA((3,)),
            pltpu.SemaphoreType.DMA((4 + 4 * depth,)),
            pltpu.SemaphoreType.DMA((4 + 4 * depth,)),
        ],
        compiler_params=pltpu.CompilerParams(
            collective_id=0, has_side_effects=True, vmem_limit_bytes=60 << 20
        ),
    )(payload, w_gate_up, w_down)


def gathered_shards(
    tokens, grad_out, routing, replica, gates, host_expert, w_gate_up, w_down
):
    devices = lax.axis_size("expert")
    features = tokens.shape[1]
    owned = w_gate_up.shape[0]
    experts = owned * devices
    lanes = (experts + 127) // 128 * 128
    picks, weights = chosen_gates(routing, replica, gates, host_expert, experts)
    side = jnp.pad(weights.astype(jnp.bfloat16), ((0, 0), (0, lanes - experts)))
    payload = jnp.concatenate([tokens, grad_out, side], axis=1)
    summed, grad_gu, grad_down = fused_layer(payload, w_gate_up, w_down, devices)
    grad_tokens = summed[:, :features]
    sums = summed[:, features : features + experts].astype(jnp.float32)
    grad_gates = jnp.sum(jnp.where(picks, sums[:, None, :], 0.0), axis=2)
    return (grad_tokens, grad_gates, grad_gu, grad_down)


def serve(tokens, grad_out, routing, replica, gates, host_expert, w_gate_up, w_down):
    squares = lax.axis_size("dp") == 4 and lax.axis_size("expert") % 2 == 0
    visits_all = routing.shape[1] >= lax.axis_size("expert")
    body = gathered_shards if squares and visits_all else shards
    return body(tokens, grad_out, routing, replica, gates, host_expert, w_gate_up, w_down)


def solution(mesh):
    in_specs = (
        P(("dp", "expert"), None),
        P(("dp", "expert"), None),
        P(("dp", "expert"), None),
        P(("dp", "expert"), None),
        P(("dp", "expert"), None),
        P(),
        P("expert", None, "dp", None),
        P("expert", "dp", None),
    )
    out_specs = (
        P(("dp", "expert"), None),
        P(("dp", "expert"), None),
        P("expert", None, "dp", None),
        P("expert", "dp", None),
    )
    return jax.shard_map(serve, mesh=mesh, in_specs=in_specs, out_specs=out_specs, check_vma=False)
```

```python
import functools

import jax
import jax.numpy as jnp
from jax import lax
from jax.experimental import pallas as pl
from jax.experimental.pallas import tpu as pltpu
from jax.sharding import PartitionSpec as P

MESH = pl.DeviceIdType.MESH


def lookup(values_table, indices):
    matches = indices[..., None] == lax.broadcasted_iota(
        jnp.int32, indices.shape + values_table.shape, indices.ndim
    )
    return jnp.sum(jnp.where(matches, values_table, 0), axis=-1)


def placement(host_expert, owned_experts, devices):
    experts = owned_experts * devices
    matches = host_expert[None, :] == lax.broadcasted_iota(jnp.int32, (experts, devices), 0)
    helper_ids = lax.broadcasted_iota(jnp.int32, (experts, devices), 1)
    helper_of = jnp.sum(jnp.where(matches, helper_ids, 0), axis=1)
    listed = jnp.sum(matches.astype(jnp.int32), axis=1)
    return (helper_of, listed)


def targets(routing, replica, host_expert, owned_experts, devices, slot_rows, groups):
    helper_of, listed = placement(host_expert, owned_experts, devices)
    choices = routing.shape[0] // groups * routing.shape[1]
    usable = (replica == 0) | (lookup(listed, routing) > 0)
    device_to = jnp.where(replica == 0, routing // owned_experts, lookup(helper_of, routing))
    block_to = jnp.where(replica == 0, routing % owned_experts, owned_experts)
    labels = (routing * 2 + replica).reshape(groups, choices)
    earlier = lax.broadcasted_iota(jnp.int32, (choices, choices), 1) < lax.broadcasted_iota(
        jnp.int32, (choices, choices), 0
    )
    matching = (labels[:, :, None] == labels[:, None, :]) & earlier[None]
    ranking = jnp.sum(matching.astype(jnp.int32), axis=2).reshape(routing.shape)
    group_ids = lax.broadcasted_iota(jnp.int32, (groups, choices), 0).reshape(routing.shape)
    position = ((block_to * groups + group_ids) * devices + device_to) * slot_rows + ranking
    return jnp.where(usable, position, -1)


def selector(position, total_slots):
    matches = position[None, :, :] == lax.broadcasted_iota(
        jnp.int32, (total_slots,) + position.shape, 0
    )
    picker = jnp.sum(matches.astype(jnp.float32), axis=2).astype(jnp.bfloat16)
    return (matches, picker)


def fill_rows(matches, picker, tokens, grad_out, gates):
    row_x = jnp.dot(picker, tokens, preferred_element_type=jnp.float32).astype(jnp.bfloat16)
    row_dy = jnp.dot(picker, grad_out, preferred_element_type=jnp.float32).astype(jnp.bfloat16)
    row_gate = jnp.sum(
        jnp.where(matches, gates[None].astype(jnp.float32), 0.0), axis=(1, 2)
    ).astype(jnp.bfloat16)
    return (row_x, row_dy, row_gate)


def expert_block(inputs, upstream, weight, gate_up, down_matrix):
    mixed = jnp.einsum("rd,jfd->jrf", inputs, gate_up, preferred_element_type=jnp.float32)
    gate_pre = mixed[0]
    up_part = mixed[1]
    sigmoid_gate = jax.nn.sigmoid(gate_pre)
    active = gate_pre * sigmoid_gate
    hidden = (active * up_part).astype(jnp.bfloat16)
    output_part = jnp.einsum("rf,fd->rd", hidden, down_matrix, preferred_element_type=jnp.float32)
    gate_part = jnp.sum(output_part * upstream.astype(jnp.float32), axis=1)
    scaled = (weight.astype(jnp.float32)[:, None] * upstream.astype(jnp.float32)).astype(
        jnp.bfloat16
    )
    grad_hidden = jnp.einsum("rd,fd->rf", scaled, down_matrix, preferred_element_type=jnp.float32)
    grad_gate = grad_hidden * up_part * sigmoid_gate * (1.0 + gate_pre * (1.0 - sigmoid_gate))
    grad_mixed = jnp.stack([grad_gate, grad_hidden * active], axis=0).astype(jnp.bfloat16)
    input_part = jnp.einsum("jrf,jfd->rd", grad_mixed, gate_up, preferred_element_type=jnp.float32)
    weight_gu = jnp.einsum("jrf,rd->jfd", grad_mixed, inputs, preferred_element_type=jnp.float32)
    weight_down = jnp.einsum("rf,rd->fd", hidden, scaled, preferred_element_type=jnp.float32)
    return (input_part, gate_part, weight_gu, weight_down)


def shards(tokens, grad_out, routing, replica, gates, host_expert, w_gate_up, w_down):
    devices = lax.axis_size("expert")
    device_id = lax.axis_index("expert")
    token_rows, features = tokens.shape
    owned_experts = w_gate_up.shape[0]
    quarter = w_down.shape[1]
    topk_width = routing.shape[1]
    slot_rows = token_rows * topk_width // (owned_experts * devices)
    blocks = owned_experts + 1
    lane_rows = devices * slot_rows
    piece_rows = quarter // devices
    home_slots = targets(routing, replica, host_expert, owned_experts, devices, slot_rows, 1)
    home_matches, home_picker = selector(home_slots, blocks * lane_rows)
    row_x, row_dy, row_gate = fill_rows(home_matches, home_picker, tokens, grad_out, gates)
    sent_x, sent_dy, sent_gate = (
        lax.all_to_all(
            row_x.reshape(blocks, lane_rows, features),
            "expert",
            split_axis=1,
            concat_axis=1,
            tiled=True,
        ),
        lax.all_to_all(
            row_dy.reshape(blocks, lane_rows, features),
            "expert",
            split_axis=1,
            concat_axis=1,
            tiled=True,
        ),
        lax.all_to_all(
            row_gate.reshape(blocks, lane_rows), "expert", split_axis=1, concat_axis=1, tiled=True
        ),
    )
    block_x, block_dy, block_gate = (
        lax.all_gather(sent_x, "dp", axis=1, tiled=True),
        lax.all_gather(sent_dy, "dp", axis=1, tiled=True),
        lax.all_gather(sent_gate, "dp", axis=1, tiled=True),
    )
    owner_of_helper = host_expert // owned_experts
    owns_copy = owner_of_helper == device_id
    copied_local = jnp.sum(jnp.where(owns_copy, host_expert % owned_experts, 0))
    helper_ids = lax.broadcasted_iota(jnp.int32, (devices, devices), 1)
    owner_ids = lax.broadcasted_iota(jnp.int32, (devices, devices), 0)
    helper_of_owner = jnp.sum(
        jnp.where(owner_of_helper[None, :] == owner_ids, helper_ids, 0), axis=1
    )
    source_gu = lax.dynamic_index_in_dim(w_gate_up, copied_local, 0, keepdims=False)
    source_down = lax.dynamic_index_in_dim(w_down, copied_local, 0, keepdims=False)
    spread_gu, spread_down = (
        lax.all_to_all(
            source_gu.reshape(2, devices, piece_rows, features),
            "expert",
            split_axis=1,
            concat_axis=1,
            tiled=True,
        ),
        lax.all_to_all(
            source_down.reshape(1, devices, piece_rows, features),
            "expert",
            split_axis=1,
            concat_axis=1,
            tiled=True,
        ),
    )
    spread_gu = jnp.take(spread_gu, owner_of_helper, axis=1)
    spread_down = jnp.take(spread_down, owner_of_helper, axis=1)
    hosted_gu, hosted_down = (
        lax.all_to_all(spread_gu, "expert", split_axis=1, concat_axis=1, tiled=True),
        lax.all_to_all(spread_down, "expert", split_axis=1, concat_axis=1, tiled=True),
    )
    hosted_gu = hosted_gu.reshape(2, quarter, features)
    hosted_down = hosted_down.reshape(quarter, features)
    input_parts = []
    gate_parts = []
    owner_gu = []
    owner_down = []
    for block in range(blocks):
        if block < owned_experts:
            gate_up = w_gate_up[block]
            down_matrix = w_down[block]
        else:
            gate_up = hosted_gu
            down_matrix = hosted_down
        input_part, gate_part, weight_gu, weight_down = expert_block(
            block_x[block], block_dy[block], block_gate[block], gate_up, down_matrix
        )
        input_parts.append(input_part.astype(jnp.bfloat16))
        gate_parts.append(gate_part.astype(jnp.bfloat16))
        owner_gu.append(weight_gu)
        owner_down.append(weight_down)
    helper_gu = owner_gu[owned_experts].astype(jnp.bfloat16)
    helper_down = owner_down[owned_experts].astype(jnp.bfloat16)
    back_gu, back_down = (
        lax.all_to_all(
            helper_gu.reshape(2, devices, piece_rows, features),
            "expert",
            split_axis=1,
            concat_axis=1,
            tiled=True,
        ),
        lax.all_to_all(
            helper_down.reshape(1, devices, piece_rows, features),
            "expert",
            split_axis=1,
            concat_axis=1,
            tiled=True,
        ),
    )
    back_gu = jnp.take(back_gu, helper_of_owner, axis=1)
    back_down = jnp.take(back_down, helper_of_owner, axis=1)
    extra_gu, extra_down = (
        lax.all_to_all(back_gu, "expert", split_axis=1, concat_axis=1, tiled=True),
        lax.all_to_all(back_down, "expert", split_axis=1, concat_axis=1, tiled=True),
    )
    extra_gu = extra_gu.reshape(2, quarter, features).astype(jnp.float32)
    extra_down = extra_down.reshape(quarter, features).astype(jnp.float32)
    stacked_dx = jnp.stack(input_parts, axis=0)
    stacked_dg = jnp.stack(gate_parts, axis=0)
    summed_dx, summed_dg = (
        lax.psum_scatter(stacked_dx, "dp", scatter_dimension=1, tiled=True).astype(jnp.float32),
        lax.psum_scatter(stacked_dg, "dp", scatter_dimension=1, tiled=True).astype(jnp.float32),
    )
    row_dx = summed_dx.astype(jnp.bfloat16)
    row_dg = summed_dg.astype(jnp.bfloat16)
    home_dx, home_dg = (
        lax.all_to_all(row_dx, "expert", split_axis=1, concat_axis=1, tiled=True),
        lax.all_to_all(row_dg, "expert", split_axis=1, concat_axis=1, tiled=True),
    )
    home_dx = home_dx.reshape(blocks * lane_rows, features)
    home_dg = home_dg.reshape(blocks * lane_rows).astype(jnp.float32)
    grad_tokens = jnp.einsum(
        "st,sd->td", home_picker, home_dx, preferred_element_type=jnp.float32
    ).astype(jnp.bfloat16)
    grad_gates = jnp.sum(jnp.where(home_matches, home_dg[:, None, None], 0.0), axis=0)
    grad_gu = []
    grad_down = []
    for block in range(owned_experts):
        present = (copied_local == block).astype(jnp.float32)
        grad_gu.append((owner_gu[block] + present * extra_gu).astype(jnp.bfloat16))
        grad_down.append((owner_down[block] + present * extra_down).astype(jnp.bfloat16))
    return (grad_tokens, grad_gates, jnp.stack(grad_gu, axis=0), jnp.stack(grad_down, axis=0))


def chosen_gates(routing, replica, gates, host_expert, experts):
    listed = jnp.any(routing[:, :, None] == host_expert[None, None, :], axis=2)
    usable = (replica == 0) | listed
    picks = usable[:, :, None] & (
        routing[:, :, None] == lax.broadcasted_iota(jnp.int32, routing.shape + (experts,), 2)
    )
    weights = jnp.sum(jnp.where(picks, gates.astype(jnp.float32)[:, :, None], 0.0), axis=1)
    return (picks, weights)


def greet(partners):
    barrier = pltpu.get_barrier_semaphore()
    for condition, device in partners:

        @pl.when(condition)
        def _():
            pl.semaphore_signal(barrier, inc=1, device_id=device, device_id_type=MESH)

    pl.semaphore_wait(barrier, sum(condition.astype(jnp.int32) for condition, _ in partners))


def fused_kernel(
    depth,
    features,
    tokens_hbm,
    upstream_hbm,
    side_hbm,
    gu_hbm,
    down_hbm,
    summed_ref,
    grad_gu_hbm,
    grad_down_hbm,
    rows_ref,
    gu_ref,
    down_ref,
    grad_gu_ref,
    grad_down_ref,
    mixed_ref,
    hidden_ref,
    part_ref,
    paired,
    ready,
    crossed,
    column_ref,
    risen,
    total,
    sent,
    landed,
    local,
    sums_sent,
    sums_landed,
):
    dp = lax.axis_index("dp")
    expert = lax.axis_index("expert")
    height, core = expert // 2, expert % 2
    row, column = dp // 2, dp % 2
    across = row * 2 + 1 - column
    along = (1 - row) * 2 + column
    diagonal = (1 - row) * 2 + 1 - column
    roles = (dp, across, along, diagonal)
    count, half = tokens_hbm.shape[0], tokens_hbm.shape[0] // 2
    owned = down_ref.shape[0]
    group_slots = 2 * depth
    group_rows = group_slots * count
    lanes = side_hbm.shape[1]
    partner = (dp, height * 2 + 1 - core)
    x_device = (across, expert)
    y_device = (along, expert)
    up_device = (dp, jnp.minimum(expert + 2, 2 * depth - 1))
    down_device = (dp, jnp.maximum(expert - 2, 0))
    has_up = height < depth - 1
    has_down = height > 0
    always = height >= 0
    levels = [lax.rem(height + step, depth) for step in range(1, depth)] + [height]
    loads = [
        pltpu.make_async_copy(gu_hbm, gu_ref, local.at[1]),
        pltpu.make_async_copy(down_hbm, down_ref, local.at[2]),
    ]
    mine = (dp * depth + height) * 2 + core
    keeps = [
        pltpu.make_async_copy(tokens_hbm, rows_ref.at[mine, :, pl.ds(0, features)], local.at[0]),
        pltpu.make_async_copy(
            upstream_hbm, rows_ref.at[mine, :, pl.ds(features, features)], local.at[3]
        ),
        pltpu.make_async_copy(
            side_hbm, rows_ref.at[mine, :, pl.ds(2 * features, lanes)], local.at[4]
        ),
    ]
    for load in keeps + loads:
        load.start()
    greet(
        [
            (always, partner),
            (always, x_device),
            (always, y_device),
            (always, (diagonal, expert)),
        ]
        + [(always, (dp, level * 2 + core)) for level in levels[:-1]]
    )

    def slot_of(dp_from, height_from, core_from):
        return (dp_from * depth + height_from) * 2 + core_from

    def copy(slot, way, device, part=None):
        block = rows_ref.at[slot]
        into = rows_ref.at[slot]
        piece = 0
        if part is not None:
            block = block.at[pl.ds(part * half, half)]
            into = into.at[pl.ds(part * half, half)]
            piece = part
        return pltpu.make_async_remote_copy(
            src_ref=block,
            dst_ref=into,
            send_sem=sent.at[slot, way * 2 + piece],
            recv_sem=landed.at[slot, piece],
            device_id=device,
            device_id_type=MESH,
        )

    finish = []

    def guard(condition, action):
        if condition is always:
            action()
        else:
            pl.when(condition)(action)

    def send(condition, *args, **kwargs):
        finish.append((condition, args, kwargs))
        guard(condition, lambda: copy(*args, **kwargs).start())

    def arrive(condition, slot, part=None):
        guard(condition, lambda: copy(slot, 0, partner, part).wait_recv())

    def both(first, second):
        return first if second is always else jnp.logical_and(first, second)

    steps = [[(always, height)]]
    for distance in range(1, depth):
        steps.append([(height >= distance, jnp.maximum(height - distance, 0))])
        steps[-1].append(
            (height + distance < depth, jnp.minimum(height + distance, depth - 1))
        )

    def relay_column(index):
        for side, (condition, level) in enumerate(steps[index]):
            slot = slot_of(dp, level, core)
            arrive(condition, slot)
            if side == 0:
                send(both(condition, has_up), slot, 3, up_device)
            else:
                send(both(condition, has_down), slot, 4, down_device)
            send(condition, slot, 1, x_device)
            send(condition, slot, 2, y_device)
            send(condition, slot, 0, partner)

    def relay_sides(index):
        for condition, level in steps[index]:
            slot = slot_of(across, level, core)
            arrive(condition, slot)
            send(condition, slot, 2, y_device, part=0)
            send(condition, slot, 0, partner)
            slot = slot_of(along, level, core)
            arrive(condition, slot)
            send(condition, slot, 1, x_device, part=1)
            send(condition, slot, 0, partner)

    def relay_diagonal(index):
        for condition, level in steps[index]:
            slot = slot_of(diagonal, level, core)
            for part in range(2):
                arrive(condition, slot, part)
                send(condition, slot, 0, partner, part=part)

    span = depth // 2
    near = height // span * span
    far = span - near

    def partner_rows(role, start=0, size=depth):
        for level in range(size):
            slot = slot_of(roles[role], start + level, 1 - core)
            if role == 3:
                arrive(always, slot, 0)
                arrive(always, slot, 1)
            else:
                arrive(always, slot)

    def remote(block, into, index, device):
        return pltpu.make_async_remote_copy(
            src_ref=block,
            dst_ref=into,
            send_sem=sums_sent.at[index],
            recv_sem=sums_landed.at[index],
            device_id=device,
            device_id_type=MESH,
        )

    def pair_copy(role, start=0, size=depth):
        return remote(
            part_ref.at[roles[role], pl.ds(start, size), 1 - core],
            paired.at[role, pl.ds(start, size)],
            role if size == depth else 4 + 4 * depth + start // span,
            partner,
        )

    def cross_copy(step, way):
        return remote(
            ready.at[step, way],
            crossed.at[step, way],
            4 + step * 3 + way,
            (roles[way + 1], expert),
        )

    def rise_copy(step):
        return remote(
            column_ref.at[step],
            risen.at[step],
            4 + 3 * depth + step,
            (dp, levels[step] * 2 + core),
        )

    def group(role, start, size):
        return pl.ds(roles[role] * group_slots + 2 * start, 2 * size)

    def rows_by_columns(a, b):
        return lax.dot_general(
            a, b, (((1,), (1,)), ((), ())), preferred_element_type=jnp.float32
        )

    def compute(role, start=0, size=depth):
        tall = size * 2 * count
        span_rows = pl.ds(pl.multiple_of(start * 2 * count, 2 * count), tall)
        inputs = rows_ref[group(role, start, size), :, :features].reshape(tall, features)
        upstream = rows_ref[group(role, start, size), :, features : 2 * features].reshape(
            tall, features
        )
        side = rows_ref[group(role, start, size), :, 2 * features :].reshape(tall, lanes)
        side = side.astype(jnp.float32)
        slots = lax.broadcasted_iota(jnp.int32, side.shape, 1)
        gate_side = jnp.zeros(side.shape, jnp.float32)
        for local_expert in range(owned):
            at_expert = slots == expert * owned + local_expert
            weight = jnp.sum(jnp.where(at_expert, side, 0.0), axis=1, keepdims=True)
            gate_pre = rows_by_columns(inputs, gu_ref[local_expert, 0])
            up_part = rows_by_columns(inputs, gu_ref[local_expert, 1])
            raw_hidden = rows_by_columns(upstream, down_ref[local_expert])
            sigmoid_gate = jax.nn.sigmoid(gate_pre)
            active = gate_pre * sigmoid_gate
            hidden = (active * up_part).astype(jnp.bfloat16).astype(jnp.float32)
            gate_part = jnp.sum(hidden * raw_hidden, axis=1, keepdims=True)
            gate_side = jnp.where(at_expert, gate_part, gate_side)
            grad_hidden = raw_hidden * weight
            grad_gate = (
                grad_hidden * up_part * sigmoid_gate * (1.0 + gate_pre * (1.0 - sigmoid_gate))
            )
            hidden_ref[local_expert, roles[role], span_rows] = (hidden * weight).astype(jnp.bfloat16)
            mixed_ref[2 * local_expert, roles[role], span_rows] = grad_gate.astype(jnp.bfloat16)
            mixed_ref[2 * local_expert + 1, roles[role], span_rows] = (grad_hidden * active).astype(
                jnp.bfloat16
            )
        dx = jnp.zeros((tall, features), jnp.float32)
        for index in range(2 * owned):
            dx = dx + jnp.dot(
                mixed_ref[index, roles[role], span_rows],
                gu_ref[index // 2, index % 2],
                preferred_element_type=jnp.float32,
            )
        shape = (size, 2, count)
        part_ref[roles[role], pl.ds(start, size), :, :, :features] = dx.astype(jnp.bfloat16).reshape(
            shape + (features,)
        )
        part_ref[roles[role], pl.ds(start, size), :, :, features:] = gate_side.astype(jnp.bfloat16).reshape(
            shape + (lanes,)
        )
        pair_copy(role, start, size).start()

    def combine(role, start=0, size=depth):
        pair_copy(role, start, size).wait_recv()
        if role > 0:
            for offset in range(size):
                level = levels[offset] if size == depth else start + offset
                step = offset if size == depth else lax.rem(level - height - 1 + depth, depth)
                ready[step, role - 1] = (
                    part_ref[roles[role], level, core].astype(jnp.float32)
                    + paired[role, level].astype(jnp.float32)
                ).astype(jnp.bfloat16)
                pltpu.make_async_remote_copy(
                    src_ref=ready.at[step, role - 1],
                    dst_ref=crossed.at[step, role - 1],
                    send_sem=sums_sent.at[4 + step * 3 + role - 1],
                    recv_sem=sums_landed.at[4 + step * 3 + role - 1],
                    device_id=(roles[role], expert),
                    device_id_type=MESH,
                ).start()

    def columns_by_columns(a, b):
        return lax.dot_general(
            a, b, (((0,), (0,)), ((), ())), preferred_element_type=jnp.float32
        ).astype(jnp.bfloat16)

    total_rows = 4 * group_rows
    quarter = mixed_ref.shape[3]

    def down_grads():
        upstream = rows_ref[:, :, features : 2 * features].reshape(total_rows, features)
        for local_expert in range(owned):
            weighted = hidden_ref[local_expert].reshape(total_rows, quarter)
            grad_down_ref[local_expert] = columns_by_columns(weighted, upstream)
        pltpu.make_async_copy(grad_down_ref, grad_down_hbm, local.at[2]).start()

    def gu_grads():
        inputs = rows_ref[:, :, :features].reshape(total_rows, features)
        for index in range(2 * owned):
            grads = mixed_ref[index].reshape(total_rows, quarter)
            grad_gu_ref[index // 2, index % 2] = columns_by_columns(grads, inputs)
        pltpu.make_async_copy(grad_gu_ref, grad_gu_hbm, local.at[1]).start()

    for keep in keeps:
        keep.wait()
    send(has_up, mine, 3, up_device)
    send(has_down, mine, 4, down_device)
    send(always, mine, 1, x_device)
    send(always, mine, 2, y_device)
    send(always, mine, 0, partner)
    for index in range(1, depth):
        relay_column(index)
        relay_sides(index - 1)
    for load in loads:
        load.wait()
    partner_rows(0)
    compute(0)
    relay_sides(depth - 1)
    relay_diagonal(0)
    partner_rows(1)
    compute(1)
    for index in range(1, span):
        relay_diagonal(index)
    partner_rows(2)
    compute(2)
    combine(0)
    combine(1)
    for index in range(span, depth - 1):
        relay_diagonal(index)
    partner_rows(3, near, span)
    compute(3, near, span)
    combine(2)
    relay_diagonal(depth - 1)
    combine(3, near, span)
    partner_rows(3, far, span)
    compute(3, far, span)
    down_grads()
    combine(3, far, span)
    gu_grads()
    for step in range(depth):
        for way in range(3):
            cross_copy(step, way).wait_recv()
        summed = part_ref[dp, levels[step], core].astype(jnp.float32) + paired[
            0, levels[step]
        ].astype(jnp.float32)
        for way in range(3):
            summed = summed + crossed[step, way].astype(jnp.float32)
        if step < depth - 1:
            column_ref[step] = summed.astype(jnp.bfloat16)
            rise_copy(step).start()
        else:
            total[...] = summed
    for step in range(depth - 1):
        rise_copy(step).wait_recv()
        total[...] = total[...] + risen[step].astype(jnp.float32)
    summed_ref[...] = total[...].astype(jnp.bfloat16)
    for condition, args, kwargs in finish:
        guard(condition, lambda args=args, kwargs=kwargs: copy(*args, **kwargs).wait_send())
    for role in range(3):
        pair_copy(role).wait_send()
    pair_copy(3, near, span).wait_send()
    pair_copy(3, far, span).wait_send()
    for step in range(depth):
        for way in range(3):
            cross_copy(step, way).wait_send()
        if step < depth - 1:
            rise_copy(step).wait_send()
    pltpu.make_async_copy(grad_down_ref, grad_down_hbm, local.at[2]).wait()
    pltpu.make_async_copy(grad_gu_ref, grad_gu_hbm, local.at[1]).wait()


def fused_layer(tokens, grad_out, side, w_gate_up, w_down, expert_size):
    count, features = tokens.shape
    width = 2 * features + side.shape[1]
    owned, quarter = w_down.shape[:2]
    depth = expert_size // 2
    slots = 4 * expert_size
    sums = width - features
    block = (count, sums)
    group_rows = expert_size * count
    kind = jnp.bfloat16
    anywhere = pl.BlockSpec(memory_space=pl.ANY)
    return pl.pallas_call(
        functools.partial(fused_kernel, depth, features),
        out_shape=(
            jax.ShapeDtypeStruct(block, kind),
            jax.ShapeDtypeStruct(w_gate_up.shape, kind),
            jax.ShapeDtypeStruct(w_down.shape, kind),
        ),
        in_specs=[anywhere] * 5,
        out_specs=(pl.BlockSpec(memory_space=pltpu.VMEM), anywhere, anywhere),
        scratch_shapes=[
            pltpu.VMEM((slots, count, width), kind),
            pltpu.VMEM(w_gate_up.shape, kind),
            pltpu.VMEM(w_down.shape, kind),
            pltpu.VMEM(w_gate_up.shape, kind),
            pltpu.VMEM(w_down.shape, kind),
            pltpu.VMEM((2 * owned, 4, group_rows, quarter), kind),
            pltpu.VMEM((owned, 4, group_rows, quarter), kind),
            pltpu.VMEM((4, depth, 2) + block, kind),
            pltpu.VMEM((4, depth) + block, kind),
            pltpu.VMEM((depth, 3) + block, kind),
            pltpu.VMEM((depth, 3) + block, kind),
            pltpu.VMEM((depth,) + block, kind),
            pltpu.VMEM((depth,) + block, kind),
            pltpu.VMEM(block, jnp.float32),
            pltpu.SemaphoreType.DMA((slots, 10)),
            pltpu.SemaphoreType.DMA((slots, 2)),
            pltpu.SemaphoreType.DMA((5,)),
            pltpu.SemaphoreType.DMA((6 + 4 * depth,)),
            pltpu.SemaphoreType.DMA((6 + 4 * depth,)),
        ],
        compiler_params=pltpu.CompilerParams(
            collective_id=0, has_side_effects=True, vmem_limit_bytes=60 << 20
        ),
    )(tokens, grad_out, side, w_gate_up, w_down)


def gathered_shards(
    tokens, grad_out, routing, replica, gates, host_expert, w_gate_up, w_down
):
    devices = lax.axis_size("expert")
    features = tokens.shape[1]
    owned = w_gate_up.shape[0]
    experts = owned * devices
    lanes = (experts + 127) // 128 * 128
    picks, weights = chosen_gates(routing, replica, gates, host_expert, experts)
    side = jnp.pad(weights.astype(jnp.bfloat16), ((0, 0), (0, lanes - experts)))
    summed, grad_gu, grad_down = fused_layer(
        tokens, grad_out, side, w_gate_up, w_down, devices
    )
    grad_tokens = summed[:, :features]
    sums = summed[:, features : features + experts].astype(jnp.float32)
    grad_gates = jnp.sum(jnp.where(picks, sums[:, None, :], 0.0), axis=2)
    return (grad_tokens, grad_gates, grad_gu, grad_down)


def serve(tokens, grad_out, routing, replica, gates, host_expert, w_gate_up, w_down):
    squares = lax.axis_size("dp") == 4 and lax.axis_size("expert") % 4 == 0
    visits_all = routing.shape[1] >= lax.axis_size("expert")
    body = gathered_shards if squares and visits_all else shards
    return body(tokens, grad_out, routing, replica, gates, host_expert, w_gate_up, w_down)


def solution(mesh):
    in_specs = (
        P(("dp", "expert"), None),
        P(("dp", "expert"), None),
        P(("dp", "expert"), None),
        P(("dp", "expert"), None),
        P(("dp", "expert"), None),
        P(),
        P("expert", None, "dp", None),
        P("expert", "dp", None),
    )
    out_specs = (
        P(("dp", "expert"), None),
        P(("dp", "expert"), None),
        P("expert", None, "dp", None),
        P("expert", "dp", None),
    )
    return jax.shard_map(serve, mesh=mesh, in_specs=in_specs, out_specs=out_specs, check_vma=False)
```
